32 devices in a mesh: groups: 1, expert: 8 (over z, core), dp: 4 (over y, x).
Axes of the slice: x: 2, y: 2, z: 4, core: 2. Of those that a mesh axis runs over, the one named last changes fastest.
Arguments:
- tokens: bfloat16 [128, 4096], P(('groups', 'expert', 'dp')), may hold values from -6 to 6
- expert_ids: int32 [128, 2], P(('groups', 'expert', 'dp')), may hold values from 0 to 7, as said below
- gate_weights: bfloat16 [128, 2], P(('groups', 'expert', 'dp')), may hold values from 0.099609375 to 1
- placement: int32 [2, 2], P('groups'), may hold values from 0 to 7, as said below
- w_gate: bfloat16 [8, 1536, 4096], P('expert', 'dp'), may hold values from -0.09375 to 0.09375
- w_up: bfloat16 [8, 1536, 4096], P('expert', 'dp'), may hold values from -0.09375 to 0.09375
- w_down: bfloat16 [8, 1536, 4096], P('expert', 'dp'), may hold values from -0.15625 to 0.15625
Outputs:
- mixed: bfloat16 [128, 4096], P(('groups', 'expert', 'dp'))
The draws below stay inside these ranges and needn't reach their ends.
Inputs may be any that keep to these rules, and one draw needn't show every extreme that they name: `expert_ids`: each row names 2 different experts. In each aligned block of 16 rows (the tokens of one index of expert) no expert is named by more than 6 rows, and some expert is named by exactly that many. `placement`: row 0 holds 2 different experts; row 1 holds 2 different expert indices, none of which appears in row 0.
All inputs are finite; a program needn't handle non-finite values.
Results may differ from the reference program's by a relative error of at most 0.015.
Values may be sent and summed in bfloat16 or wider, within the bound.
No kernel may reach another device: no remote copies, remote signals or barrier semaphores. Data moves between devices by JAX's collectives and lax.ppermute only.
A program may use at most 64 MiB of HBM per device.

```python
import math
import jax
import jax.numpy as jnp
from jax import lax

D = 4096
FF = 1536
HOT = 2
EXPERTS = 8
TOPK = 2
GROUP = 16
TOKENS = 128
CAP = 4
OVF = 2
N_EXPERT = 8
N_DP = 4


def listed_pairs(key):
    others = jax.random.permutation(jax.random.fold_in(key, 11), EXPERTS - 1).astype(jnp.int32)
    picked = others[:2 * HOT]
    position = jax.random.randint(jax.random.fold_in(key, 13), (), 0, 2 * HOT).astype(jnp.int32)
    slot_iota = jnp.arange(2 * HOT, dtype=jnp.int32)
    picked = jnp.where(slot_iota == position, EXPERTS - 1, picked).astype(jnp.int32)
    return (picked[:HOT], picked[HOT:2 * HOT])


def draw_placement(key, part):
    chosen, owners = listed_pairs(key)
    return jnp.stack([chosen, owners]).astype(jnp.int32)


def route_block(key, chosen, block_index):
    slots = CAP + OVF
    total = GROUP * TOPK
    block_key = jax.random.fold_in(jax.random.fold_in(key, 23), block_index)
    shuffled = jax.random.permutation(jax.random.fold_in(block_key, 1), EXPERTS).astype(jnp.int32)
    experts_iota = jnp.arange(EXPERTS, dtype=jnp.int32)
    is_listed = jnp.any(experts_iota[:, None] == chosen[None, :], axis=1)
    score = jnp.where(is_listed, 0, 1 + shuffled).astype(jnp.int32)
    order = jnp.argsort(score, stable=True).astype(jnp.int32)
    counts = jnp.clip(total - experts_iota * slots, 0, slots).astype(jnp.int32)
    ends = jnp.cumsum(counts).astype(jnp.int32)
    pair_iota = jnp.arange(total, dtype=jnp.int32)
    which = jnp.sum((pair_iota[:, None] >= ends[None, :]).astype(jnp.int32), axis=1)
    named = order[which]
    grid = named.reshape(TOPK, GROUP).T
    row_order = jax.random.permutation(jax.random.fold_in(block_key, 2), GROUP)
    return grid[row_order].astype(jnp.int32)


def draw_expert_ids(key, part):
    chosen, owners = listed_pairs(key)
    blocks = jax.vmap(lambda index: route_block(key, chosen, index))(jnp.arange(N_EXPERT, dtype=jnp.int32))
    return blocks.reshape(TOKENS, TOPK).astype(jnp.int32)


def level_of(own_key, shape, cuts, low, high):
    gain = 1.0
    for dim, blocks in cuts:
        draws = jax.random.uniform(jax.random.fold_in(jax.random.fold_in(own_key, 6), dim), (blocks,), jnp.float32, low / len(cuts), high / len(cuts))
        gain = gain * jnp.repeat(jnp.exp(draws), shape[dim] // blocks).reshape((-1,) + (1,) * (len(shape) - 1 - dim))
    return gain


def scatter_about(key, dims, width, reach, cuts=(), kind=jnp.bfloat16):
    array = jax.random.normal(key, dims, jnp.float32) * width
    if len(cuts) > 0:
        array = level_of(key, dims, cuts, -0.22, 0.18) * array
    return jnp.clip(array, min=-reach, max=reach).astype(kind)


def setup_inputs(seed: int = 0, part: int = 0) -> dict:
    key_list = jax.random.split(jax.random.key(seed), 8)
    part_keys = jax.random.split(jax.random.fold_in(key_list[7], part), 8)
    return {
        "tokens": scatter_about(part_keys[0], (TOKENS, D), 1.0, 6.0, ((0, 32),)),
        "expert_ids": draw_expert_ids(jax.random.fold_in(jax.random.fold_in(key_list[7], part), 71), part),
        "gate_weights": jnp.clip(jnp.exp(math.log(1.0) - 2.306499 * jax.random.uniform(part_keys[2], (TOKENS, TOPK), jnp.float32) ** level_of(part_keys[2], (TOKENS, TOPK), ((0, 32),), -0.2, 0.2)), 0.099609375, 1.0).astype(jnp.bfloat16),
        "placement": draw_placement(jax.random.fold_in(jax.random.fold_in(key_list[7], part), 71), part),
        "w_gate": scatter_about(key_list[4], (EXPERTS, FF, D), D ** -0.5, 0.09375, ((0, 8), (1, 4))),
        "w_up": scatter_about(key_list[5], (EXPERTS, FF, D), D ** -0.5, 0.09375, ((0, 8), (1, 4))),
        "w_down": scatter_about(key_list[6], (EXPERTS, FF, D), FF ** -0.5, 0.15625, ((0, 8), (1, 4))),
    }


def reference(tokens, expert_ids, gate_weights, placement, w_gate, w_up, w_down):
    slots = CAP + OVF
    pairs = GROUP * TOPK
    flat_ids = expert_ids.reshape(N_EXPERT, pairs)
    onehot = (flat_ids[:, :, None] == jnp.arange(EXPERTS, dtype=jnp.int32)[None, None, :]).astype(jnp.int32)
    before = jnp.cumsum(onehot, axis=1) - onehot
    rank = jnp.sum(before * onehot, axis=2)
    listed = jnp.any(flat_ids[:, :, None] == placement[0][None, None, :], axis=2)
    keep = (rank < CAP) | (listed & (rank < slots))
    group_index = jnp.arange(N_EXPERT, dtype=jnp.int32)[:, None]
    total_rows = EXPERTS * N_EXPERT * slots
    row = flat_ids * (N_EXPERT * slots) + group_index * slots + rank
    row = jnp.where(keep, row, total_rows).astype(jnp.int32).reshape(-1)
    token_index = (group_index * GROUP + jnp.arange(pairs, dtype=jnp.int32)[None, :] // TOPK).astype(jnp.int32).reshape(-1)
    table = jnp.zeros((total_rows + 1,), jnp.int32).at[row].set(token_index)[:-1]
    weight_table = jnp.zeros((total_rows + 1,), jnp.float32).at[row].set(gate_weights.astype(jnp.float32).reshape(-1))[:-1]
    table = table.reshape(EXPERTS, N_EXPERT * slots)
    block = FF // N_DP
    contract = (((1,), (1,)), ((), ()))

    def expert(args):
        index, gate_w, up_w, down_w = args
        rows = tokens[index]
        gate = lax.dot_general(rows, gate_w, contract, preferred_element_type=jnp.float32)
        up = lax.dot_general(rows, up_w, contract, preferred_element_type=jnp.float32)
        hidden = (jax.nn.silu(gate) * up).astype(jnp.bfloat16)
        pieces = jnp.einsum("rbf,bfd->rbd", hidden.reshape(-1, N_DP, block).astype(jnp.float32),
                            down_w.reshape(N_DP, block, D).astype(jnp.float32))
        pieces = pieces.astype(jnp.bfloat16).astype(jnp.float32)
        return jnp.sum(pieces, axis=1)

    results = lax.map(expert, (table, w_gate, w_up, w_down))
    weighted = results.reshape(total_rows, D) * weight_table[:, None]
    mixed = jnp.zeros((TOKENS, D), jnp.float32).at[table.reshape(-1)].add(weighted)
    return mixed.astype(jnp.bfloat16)
```

```python
import functools

import jax
import jax.numpy as jnp
from jax import lax
from jax.experimental import pallas as pl
from jax.experimental.pallas import tpu as pltpu
from jax.sharding import PartitionSpec as P

BF16, F32, I32 = jnp.bfloat16, jnp.float32, jnp.int32
CHUNKS = 8
LANES = 128


def iota(shape, dim):
    return lax.broadcasted_iota(I32, shape, dim)


def onehot(cond):
    return jnp.where(cond, 1.0, 0.0).astype(BF16)


def mm(a, b, contract=((1,), (0,))):
    return lax.dot_general(a, b, (contract, ((), ())), preferred_element_type=F32)


def dot(a, b, contract=((1,), (0,))):
    return mm(a.astype(BF16), b.astype(BF16), contract)


def partner(me, step, n):
    if n & (n - 1) == 0:
        return me ^ step
    return (step + n - me) % n


def swap(x, axis, step, n):
    return lax.ppermute(x, axis, [(i, partner(i, step, n)) for i in range(n)])


def pack_kernel(n_dp, tok_ref, ids_ref, gate_ref, out_ref):
    count, width = tok_ref.shape
    topk = ids_ref.shape[0]
    lanes = width // CHUNKS
    rows = count * CHUNKS
    extra = out_ref.shape[0] - rows
    me = lax.axis_index("dp")
    acc = jnp.zeros((rows, lanes), F32)
    row, col = iota((rows, count), 0), iota((rows, count), 1)
    for c in range(CHUNKS):
        pick = onehot(row == col * CHUNKS + c)
        acc += mm(pick, tok_ref[:, c * lanes:(c + 1) * lanes])
    out_ref[:rows, :] = acc.astype(BF16)
    place = onehot(iota((count, lanes), 1) == iota((count, lanes), 0) + me * count)
    ids_row = onehot(iota((extra, topk), 0) == iota((extra, topk), 1))
    gate_row = onehot(iota((extra, topk), 0) == iota((extra, topk), 1) + topk)
    small = dot(ids_row, (ids_ref[...] + 1).astype(F32)) + dot(gate_row, gate_ref[...])
    out_ref[rows:, :] = dot(small, place).astype(BF16)


def select_kernel(n_expert, n_dp, first, slots, topk, *refs):
    place_ref, blocks = refs[0], refs[1:1 + n_dp]
    send_ref, mix_ref, group_ref = refs[1 + n_dp:]
    lanes = send_ref.shape[1]
    per = group_ref.shape[0] // n_dp
    count = per // CHUNKS
    total = send_ref.shape[0]
    me = lax.axis_index("dp")
    small = None
    for j, ref in enumerate(blocks):
        group_ref[j * per:(j + 1) * per, :] = ref[:per, :]
        part = ref[per:, :LANES].astype(F32)
        small = part if small is None else small + part
    row = iota((total, LANES), 0)
    pair_row = (row // CHUNKS).astype(F32)
    expert = jnp.floor((pair_row + 0.5) * (1.0 / slots))
    slot = pair_row - expert * slots
    named = jnp.zeros((total, LANES), F32)
    gate = jnp.zeros((total, LANES), F32)
    for k in range(topk):
        hit = small[k:k + 1, :] == expert + 1.0
        named = jnp.where(hit, 1.0, named)
        gate = jnp.where(hit, small[topk + k:topk + k + 1, :], gate)
    earlier = onehot(iota((LANES, LANES), 0) < iota((LANES, LANES), 1))
    rank = dot(named, earlier)
    allowed = slot < first
    for h in range(place_ref.shape[1]):
        allowed |= expert == place_ref[0, h].astype(F32)
    chosen = jnp.where(allowed & (rank == slot), named, 0.0)
    group_rows = n_dp * per
    at = iota((LANES, group_rows), 1)
    source = partner(me, at // per, n_dp)
    token = source * count + (at % per) // CHUNKS
    spread = onehot(iota((LANES, group_rows), 0) == token)
    same = iota((total, group_rows), 0) % CHUNKS == iota((total, group_rows), 1) % CHUNKS
    pick = jnp.where(same, dot(chosen, spread), 0.0).astype(BF16)
    mix_ref[...] = jnp.where(same, dot(chosen * gate, spread), 0.0).astype(BF16)
    send_ref[...] = mm(pick, group_ref[...]).astype(BF16)


def expert_kernel(rows_ref, gate_ref, up_ref, down_ref, out_ref, x_ref, y_ref):
    total, lanes = rows_ref.shape
    count = total // CHUNKS
    nt = ((1,), (1,))
    tn = ((0,), (0,))
    row, col = iota((count, total), 0), iota((count, total), 1)
    for c in range(CHUNKS):
        pick = onehot(col == row * CHUNKS + c)
        x_ref[:, c * lanes:(c + 1) * lanes] = mm(pick, rows_ref[...]).astype(BF16)
    gate = mm(x_ref[...], gate_ref[...], nt)
    up = mm(x_ref[...], up_ref[...], nt)
    hidden = (gate / (1.0 + jnp.exp(-gate)) * up).astype(BF16)
    for c in range(CHUNKS):
        value = mm(hidden, down_ref[:, c * lanes:(c + 1) * lanes]).astype(BF16)
        y_ref[c * count:(c + 1) * count, :] = value
    row, col = iota((total, total), 0), iota((total, total), 1)
    order = onehot(row == (col % count) * CHUNKS + col // count)
    out_ref[...] = mm(order, y_ref[...]).astype(BF16)


def mix_kernel(back_ref, mix_ref, *out_refs):
    value = mm(mix_ref[...], back_ref[...], ((0,), (0,))).astype(BF16)
    per = out_refs[0].shape[0]
    for j, ref in enumerate(out_refs):
        ref[...] = value[j * per:(j + 1) * per, :]


def finish_kernel(*refs):
    out_ref = refs[-1]
    total = refs[0][...].astype(F32)
    for ref in refs[1:-1]:
        total += ref[...].astype(F32)
    total = total.astype(BF16)
    rows, lanes = total.shape
    count = out_ref.shape[0]
    row, col = iota((count, rows), 0), iota((count, rows), 1)
    for c in range(CHUNKS):
        pick = onehot(col == row * CHUNKS + c)
        out_ref[:, c * lanes:(c + 1) * lanes] = mm(pick, total).astype(BF16)


def call(kernel, out_shape, in_specs=None, scratch=(), limit=8 << 20, **kw):
    return pl.pallas_call(
        kernel,
        out_shape=out_shape,
        scratch_shapes=scratch,
        compiler_params=pltpu.CompilerParams(vmem_limit_bytes=limit),
        **({} if in_specs is None else {"in_specs": in_specs}),
        **kw,
    )


def body(tokens, expert_ids, gate_weights, placement, w_gate, w_up, w_down):
    n_expert, n_dp = lax.axis_size("expert"), lax.axis_size("dp")
    count, width = tokens.shape
    topk = expert_ids.shape[1]
    group = count * n_dp
    assert group <= LANES and n_expert < 256 and width % (CHUNKS * LANES) == 0
    first = max(2, group * topk // n_expert)
    slots = first + max(1, first // 2)
    lanes = width // CHUNKS
    per = count * CHUNKS
    extra = -(-2 * topk // 8) * 8
    total = n_expert * slots * CHUNKS
    shape = lambda *dims: jax.ShapeDtypeStruct(dims, BF16)
    vmem = pl.BlockSpec(memory_space=pltpu.VMEM)
    smem = pl.BlockSpec(memory_space=pltpu.SMEM)

    packed = call(functools.partial(pack_kernel, n_dp), shape(per + extra, lanes))(
        tokens, expert_ids.T, gate_weights.T
    )
    blocks = [packed] + [swap(packed, "dp", j, n_dp) for j in range(1, n_dp)]
    send, mix = call(
        functools.partial(select_kernel, n_expert, n_dp, first, slots, topk),
        (shape(total, lanes), shape(total, n_dp * per)),
        [smem] + [vmem] * n_dp,
        (pltpu.VMEM((n_dp * per, lanes), BF16),),
        limit=40 << 20 if total > 1024 else 8 << 20,
    )(placement, *blocks)
    received = lax.all_to_all(
        send.reshape(n_expert, -1, lanes), "expert", split_axis=0, concat_axis=0, tiled=True
    )
    partial_rows = call(
        expert_kernel,
        shape(total, lanes),
        scratch=(
            pltpu.VMEM((total // CHUNKS, width), BF16),
            pltpu.VMEM((total, lanes), BF16),
        ),
        limit=60 << 20 if total > 1024 else 24 << 20,
    )(received.reshape(total, lanes), w_gate[0], w_up[0], w_down[0])
    back = lax.all_to_all(
        partial_rows.reshape(n_expert, -1, lanes), "expert", split_axis=0, concat_axis=0, tiled=True
    )
    outs = call(mix_kernel, [shape(per, lanes)] * n_dp, limit=24 << 20)(
        back.reshape(total, lanes), mix
    )
    pieces = [outs[0]] + [swap(outs[j], "dp", j, n_dp) for j in range(1, n_dp)]
    return call(finish_kernel, shape(count, width))(*pieces)


def solution(mesh):
    placed = (
        P(("groups", "expert", "dp"), None),
        P(("groups", "expert", "dp"), None),
        P(("groups", "expert", "dp"), None),
        P("groups", None),
        P("expert", "dp", None),
        P("expert", "dp", None),
        P("expert", "dp", None),
    )
    return jax.shard_map(
        body,
        mesh=mesh,
        in_specs=placed,
        out_specs=P(("groups", "expert", "dp"), None),
        check_vma=False,
    )
```

```python
import functools

import jax
import jax.numpy as jnp
from jax import lax
from jax.experimental import pallas as pl
from jax.experimental.pallas import tpu as pltpu
from jax.sharding import PartitionSpec as P

BF16, F32, I32 = jnp.bfloat16, jnp.float32, jnp.int32
CHUNKS = 8
LANES = 128


def iota(shape, dim):
    return lax.broadcasted_iota(I32, shape, dim)


def onehot(cond):
    return jnp.where(cond, 1.0, 0.0).astype(BF16)


def mm(a, b, contract=((1,), (0,))):
    return lax.dot_general(a, b, (contract, ((), ())), preferred_element_type=F32)


def dot(a, b, contract=((1,), (0,))):
    return mm(a.astype(BF16), b.astype(BF16), contract)


def partner(me, step, n):
    if n & (n - 1) == 0:
        return me ^ step
    return (step + n - me) % n


def swap(x, axis, step, n):
    return lax.ppermute(x, axis, [(i, partner(i, step, n)) for i in range(n)])


def pack_kernel(tok_hbm, ids_hbm, gate_hbm, place_hbm, out_ref, tok_ref, ids_ref, gate_ref, place_ref, sems):
    pairs = ((ids_hbm, ids_ref), (gate_hbm, gate_ref), (place_hbm, place_ref), (tok_hbm, tok_ref))
    copies = [pltpu.make_async_copy(a, b, sems.at[i]) for i, (a, b) in enumerate(pairs)]
    for copy in copies:
        copy.start()
    count, width = tok_ref.shape
    topk = ids_ref.shape[0]
    lanes = width // CHUNKS
    rows = count * CHUNKS
    extra = out_ref.shape[0] - rows
    me = lax.axis_index("dp")
    place = onehot(iota((count, LANES), 1) == iota((count, LANES), 0) + me * count)
    ids_row = onehot(iota((extra, topk), 0) == iota((extra, topk), 1))
    gate_row = onehot(iota((extra, topk), 0) == iota((extra, topk), 1) + topk)
    for copy in copies[:3]:
        copy.wait()
    small = dot(ids_row, (ids_ref[...] + 1).astype(F32)) + dot(gate_row, gate_ref[...])
    out_ref[rows:, :LANES] = dot(small, place).astype(BF16)
    line = iota((extra, LANES), 0)
    listed = jnp.zeros((extra, LANES), F32)
    for h in range(place_ref.shape[1]):
        listed = jnp.where(line == h, (place_ref[0:1, h:h + 1] + 1).astype(F32), listed)
    out_ref[rows:, LANES:2 * LANES] = listed.astype(BF16)
    out_ref[rows:, 2 * LANES:] = jnp.zeros((extra, lanes - 2 * LANES), BF16)
    acc = jnp.zeros((rows, lanes), F32)
    row, col = iota((rows, count), 0), iota((rows, count), 1)
    copies[3].wait()
    for c in range(CHUNKS):
        pick = onehot(row == col * CHUNKS + c)
        acc += mm(pick, tok_ref[:, c * lanes:(c + 1) * lanes])
    out_ref[:rows, :] = acc.astype(BF16)


def select_kernel(n_expert, n_dp, first, slots, topk, hot, *refs):
    blocks, sends = refs[:n_dp], refs[n_dp:n_dp + n_expert]
    mix_ref, group_ref = refs[n_dp + n_expert:]
    lanes = group_ref.shape[1]
    per = group_ref.shape[0] // n_dp
    count = per // CHUNKS
    piece = slots * CHUNKS
    total = n_expert * piece
    me = lax.axis_index("dp")
    small = None
    for j, ref in enumerate(blocks):
        group_ref[j * per:(j + 1) * per, :] = ref[:per, :]
        part = ref[per:, :LANES].astype(F32)
        small = part if small is None else small + part
    places = blocks[0][per:, LANES:2 * LANES].astype(F32)
    row = iota((total, LANES), 0)
    step = row // piece
    expert = partner(lax.axis_index("expert"), step, n_expert).astype(F32)
    slot = ((row - step * piece) // CHUNKS).astype(F32)
    named = jnp.zeros((total, LANES), F32)
    gate = jnp.zeros((total, LANES), F32)
    for k in range(topk):
        hit = small[k:k + 1, :] == expert + 1.0
        named = jnp.where(hit, 1.0, named)
        gate = jnp.where(hit, small[topk + k:topk + k + 1, :], gate)
    earlier = onehot(iota((LANES, LANES), 0) < iota((LANES, LANES), 1))
    rank = dot(named, earlier)
    allowed = slot < first
    for h in range(hot):
        allowed |= expert + 1.0 == places[h:h + 1, :]
    chosen = jnp.where(allowed & (rank == slot), named, 0.0)
    group_rows = n_dp * per
    at = iota((LANES, group_rows), 1)
    source = partner(me, at // per, n_dp)
    token = source * count + (at % per) // CHUNKS
    spread = onehot(iota((LANES, group_rows), 0) == token)
    same = iota((total, group_rows), 0) % CHUNKS == iota((total, group_rows), 1) % CHUNKS
    pick = jnp.where(same, dot(chosen, spread), 0.0).astype(BF16)
    value = mm(pick, group_ref[...]).astype(BF16)
    for j, ref in enumerate(sends):
        ref[...] = value[j * piece:(j + 1) * piece, :]
    mix_ref[...] = jnp.where(same, dot(chosen * gate, spread), 0.0).astype(BF16)


def expert_kernel(n_expert, *refs):
    ins, outs = refs[:n_expert], refs[n_expert + 3:2 * n_expert + 3]
    gate_ref, up_ref, down_ref = refs[n_expert:n_expert + 3]
    x_ref, y_ref = refs[2 * n_expert + 3:]
    total, lanes = y_ref.shape
    piece = total // n_expert
    count = total // CHUNKS
    nt = ((1,), (1,))
    for j, ref in enumerate(ins):
        y_ref[j * piece:(j + 1) * piece, :] = ref[...]
    row, col = iota((count, total), 0), iota((count, total), 1)
    for c in range(CHUNKS):
        pick = onehot(col == row * CHUNKS + c)
        x_ref[:, c * lanes:(c + 1) * lanes] = mm(pick, y_ref[...]).astype(BF16)
    gate = mm(x_ref[...], gate_ref[...], nt)
    up = mm(x_ref[...], up_ref[...], nt)
    hidden = (gate / (1.0 + jnp.exp(-gate)) * up).astype(BF16)
    for c in range(CHUNKS):
        value = mm(hidden, down_ref[:, c * lanes:(c + 1) * lanes]).astype(BF16)
        y_ref[c * count:(c + 1) * count, :] = value
    row, col = iota((piece, total), 0), iota((piece, total), 1)
    for j, ref in enumerate(outs):
        order = onehot(row + j * piece == (col % count) * CHUNKS + col // count)
        ref[...] = mm(order, y_ref[...]).astype(BF16)


def mix_kernel(n_expert, *refs):
    backs, mix_ref, out_refs = refs[:n_expert], refs[n_expert], refs[n_expert + 1:-1]
    rows_ref = refs[-1]
    piece = backs[0].shape[0]
    for j, ref in enumerate(backs):
        rows_ref[j * piece:(j + 1) * piece, :] = ref[...]
    value = mm(mix_ref[...], rows_ref[...], ((0,), (0,))).astype(BF16)
    per = out_refs[0].shape[0]
    for j, ref in enumerate(out_refs):
        ref[...] = value[j * per:(j + 1) * per, :]


def finish_kernel(*refs):
    out_ref = refs[-1]
    total = refs[0][...].astype(F32)
    for ref in refs[1:-1]:
        total += ref[...].astype(F32)
    total = total.astype(BF16)
    rows, lanes = total.shape
    count = out_ref.shape[0]
    row, col = iota((count, rows), 0), iota((count, rows), 1)
    for c in range(CHUNKS):
        pick = onehot(col == row * CHUNKS + c)
        out_ref[:, c * lanes:(c + 1) * lanes] = mm(pick, total).astype(BF16)


def call(kernel, out_shape, in_specs=None, scratch=(), limit=8 << 20, **kw):
    return pl.pallas_call(
        kernel,
        out_shape=out_shape,
        scratch_shapes=scratch,
        compiler_params=pltpu.CompilerParams(vmem_limit_bytes=limit),
        **({} if in_specs is None else {"in_specs": in_specs}),
        **kw,
    )


def body(tokens, expert_ids, gate_weights, placement, w_gate, w_up, w_down):
    n_expert, n_dp = lax.axis_size("expert"), lax.axis_size("dp")
    count, width = tokens.shape
    topk = expert_ids.shape[1]
    group = count * n_dp
    assert group <= LANES and n_expert < 256 and width % (CHUNKS * LANES) == 0
    assert width >= 2 * CHUNKS * LANES and placement.shape[1] <= 8
    first = max(2, group * topk // n_expert)
    slots = first + max(1, first // 2)
    lanes = width // CHUNKS
    per = count * CHUNKS
    extra = -(-2 * topk // 8) * 8
    total = n_expert * slots * CHUNKS
    shape = lambda *dims: jax.ShapeDtypeStruct(dims, BF16)
    hbm = pl.BlockSpec(memory_space=pltpu.HBM)
    big = total > 1024

    packed = call(
        pack_kernel,
        shape(per + extra, lanes),
        [hbm] * 4,
        (
            pltpu.VMEM((count, width), BF16),
            pltpu.VMEM((topk, count), I32),
            pltpu.VMEM((topk, count), BF16),
            pltpu.VMEM(placement.shape, I32),
            pltpu.SemaphoreType.DMA((4,)),
        ),
    )(tokens, expert_ids.T, gate_weights.T, placement)
    blocks = [packed] + [swap(packed, "dp", j, n_dp) for j in range(1, n_dp)]
    hot = placement.shape[1]
    *sends, mix = call(
        functools.partial(select_kernel, n_expert, n_dp, first, slots, topk, hot),
        [shape(slots * CHUNKS, lanes)] * n_expert + [shape(total, n_dp * per)],
        scratch=(pltpu.VMEM((n_dp * per, lanes), BF16),),
        limit=40 << 20 if big else 8 << 20,
    )(*blocks)
    rows = [sends[0]] + [swap(sends[j], "expert", j, n_expert) for j in range(1, n_expert)]
    parts = call(
        functools.partial(expert_kernel, n_expert),
        [shape(slots * CHUNKS, lanes)] * n_expert,
        scratch=(
            pltpu.VMEM((total // CHUNKS, width), BF16),
            pltpu.VMEM((total, lanes), BF16),
        ),
        limit=60 << 20 if big else 24 << 20,
    )(*rows, w_gate[0], w_up[0], w_down[0])
    backs = [parts[0]] + [swap(parts[j], "expert", j, n_expert) for j in range(1, n_expert)]
    outs = call(
        functools.partial(mix_kernel, n_expert),
        [shape(per, lanes)] * n_dp,
        scratch=(pltpu.VMEM((total, lanes), BF16),),
        limit=24 << 20 if big else 8 << 20,
    )(*backs, mix)
    pieces = [outs[0]] + [swap(outs[j], "dp", j, n_dp) for j in range(1, n_dp)]
    return call(finish_kernel, shape(count, width))(*pieces)


def solution(mesh):
    placed = (
        P(("groups", "expert", "dp"), None),
        P(("groups", "expert", "dp"), None),
        P(("groups", "expert", "dp"), None),
        P("groups", None),
        P("expert", "dp", None),
        P("expert", "dp", None),
        P("expert", "dp", None),
    )
    return jax.shard_map(
        body,
        mesh=mesh,
        in_specs=placed,
        out_specs=P(("groups", "expert", "dp"), None),
        check_vma=False,
    )
```

```python
import functools

import jax
import jax.numpy as jnp
from jax import lax
from jax.experimental import pallas as pl
from jax.experimental.pallas import tpu as pltpu
from jax.sharding import PartitionSpec as P

BF16, F32, I32 = jnp.bfloat16, jnp.float32, jnp.int32
CHUNKS = 8
LANES = 128


def iota(shape, dim):
    return lax.broadcasted_iota(I32, shape, dim)


def onehot(cond):
    return jnp.where(cond, 1.0, 0.0).astype(BF16)


def mm(a, b, contract=((1,), (0,))):
    return lax.dot_general(a, b, (contract, ((), ())), preferred_element_type=F32)


def dot(a, b, contract=((1,), (0,))):
    return mm(a.astype(BF16), b.astype(BF16), contract)


def partner(me, step, n):
    if n & (n - 1) == 0:
        return me ^ step
    return (step + n - me) % n


def swap(x, axis, step, n):
    return lax.ppermute(x, axis, [(i, partner(i, step, n)) for i in range(n)])


def pack_kernel(tok_hbm, ids_hbm, gate_hbm, place_hbm, out_ref, tok_ref, ids_ref, gate_ref, place_ref, sems):
    pairs = ((ids_hbm, ids_ref), (gate_hbm, gate_ref), (place_hbm, place_ref), (tok_hbm, tok_ref))
    copies = [pltpu.make_async_copy(a, b, sems.at[i]) for i, (a, b) in enumerate(pairs)]
    for copy in copies:
        copy.start()
    count, width = tok_ref.shape
    topk = ids_ref.shape[0]
    lanes = width // CHUNKS
    rows = count * CHUNKS
    extra = out_ref.shape[0] - rows
    me = lax.axis_index("dp")
    place = onehot(iota((count, LANES), 1) == iota((count, LANES), 0) + me * count)
    ids_row = onehot(iota((extra, topk), 0) == iota((extra, topk), 1))
    gate_row = onehot(iota((extra, topk), 0) == iota((extra, topk), 1) + topk)
    for copy in copies[:3]:
        copy.wait()
    small = dot(ids_row, (ids_ref[...] + 1).astype(F32)) + dot(gate_row, gate_ref[...])
    out_ref[rows:, :LANES] = dot(small, place).astype(BF16)
    line = iota((extra, LANES), 0)
    listed = jnp.zeros((extra, LANES), F32)
    for h in range(place_ref.shape[1]):
        listed = jnp.where(line == h, (place_ref[0:1, h:h + 1] + 1).astype(F32), listed)
    out_ref[rows:, LANES:2 * LANES] = listed.astype(BF16)
    out_ref[rows:, 2 * LANES:] = jnp.zeros((extra, lanes - 2 * LANES), BF16)
    acc = jnp.zeros((rows, lanes), F32)
    row, col = iota((rows, count), 0), iota((rows, count), 1)
    copies[3].wait()
    for c in range(CHUNKS):
        pick = onehot(row == col * CHUNKS + c)
        acc += mm(pick, tok_ref[:, c * lanes:(c + 1) * lanes])
    out_ref[:rows, :] = acc.astype(BF16)


def select_kernel(n_expert, n_dp, first, slots, topk, hot, *refs):
    blocks, sends = refs[:n_dp], refs[n_dp:n_dp + n_expert]
    mix_ref, group_ref = refs[n_dp + n_expert:]
    lanes = group_ref.shape[1]
    per = group_ref.shape[0] // n_dp
    count = per // CHUNKS
    piece = slots * CHUNKS
    total = n_expert * piece
    me = lax.axis_index("dp")
    small = None
    for j, ref in enumerate(blocks):
        group_ref[j * per:(j + 1) * per, :] = ref[:per, :]
        part = ref[per:, :LANES].astype(F32)
        small = part if small is None else small + part
    places = blocks[0][per:, LANES:2 * LANES].astype(F32)
    row = iota((total, LANES), 0)
    step = row // piece
    expert = partner(lax.axis_index("expert"), step, n_expert).astype(F32)
    slot = ((row - step * piece) // CHUNKS).astype(F32)
    named = jnp.zeros((total, LANES), F32)
    gate = jnp.zeros((total, LANES), F32)
    for k in range(topk):
        hit = small[k:k + 1, :] == expert + 1.0
        named = jnp.where(hit, 1.0, named)
        gate = jnp.where(hit, small[topk + k:topk + k + 1, :], gate)
    earlier = onehot(iota((LANES, LANES), 0) < iota((LANES, LANES), 1))
    rank = dot(named, earlier)
    allowed = slot < first
    for h in range(hot):
        allowed |= expert + 1.0 == places[h:h + 1, :]
    chosen = jnp.where(allowed & (rank == slot), named, 0.0)
    group_rows = n_dp * per
    at = iota((LANES, group_rows), 1)
    source = partner(me, at // per, n_dp)
    token = source * count + (at % per) // CHUNKS
    spread = onehot(iota((LANES, group_rows), 0) == token)
    same = iota((total, group_rows), 0) % CHUNKS == iota((total, group_rows), 1) % CHUNKS
    pick = jnp.where(same, dot(chosen, spread), 0.0).astype(BF16)
    value = mm(pick, group_ref[...]).astype(BF16)
    for j, ref in enumerate(sends):
        ref[...] = value[j * piece:(j + 1) * piece, :]
    mix_ref[...] = jnp.where(same, dot(chosen * gate, spread), 0.0).astype(BF16)


def expert_kernel(n_expert, *refs):
    ins, outs = refs[:n_expert], refs[n_expert + 3:2 * n_expert + 3]
    gate_ref, up_ref, down_ref = refs[n_expert:n_expert + 3]
    x_ref, y_ref = refs[2 * n_expert + 3:]
    total, lanes = y_ref.shape
    piece = total // n_expert
    count = total // CHUNKS
    nt = ((1,), (1,))
    for j, ref in enumerate(ins):
        y_ref[j * piece:(j + 1) * piece, :] = ref[...]
    row, col = iota((count, total), 0), iota((count, total), 1)
    for c in range(CHUNKS):
        pick = onehot(col == row * CHUNKS + c)
        x_ref[:, c * lanes:(c + 1) * lanes] = mm(pick, y_ref[...]).astype(BF16)
    gate = mm(x_ref[...], gate_ref[...], nt)
    up = mm(x_ref[...], up_ref[...], nt)
    hidden = (gate / (1.0 + jnp.exp(-gate)) * up).astype(BF16)
    for c in range(CHUNKS):
        value = mm(hidden, down_ref[:, c * lanes:(c + 1) * lanes]).astype(BF16)
        y_ref[c * count:(c + 1) * count, :] = value
    row, col = iota((piece, total), 0), iota((piece, total), 1)
    for j, ref in enumerate(outs):
        order = onehot(row + j * piece == (col % count) * CHUNKS + col // count)
        ref[...] = mm(order, y_ref[...]).astype(BF16)


def mix_kernel(n_expert, *refs):
    backs, mix_ref, out_refs = refs[:n_expert], refs[n_expert], refs[n_expert + 1:-1]
    rows_ref = refs[-1]
    piece = backs[0].shape[0]
    for j, ref in enumerate(backs):
        rows_ref[j * piece:(j + 1) * piece, :] = ref[...]
    value = mm(mix_ref[...], rows_ref[...], ((0,), (0,))).astype(BF16)
    per = out_refs[0].shape[0]
    for j, ref in enumerate(out_refs):
        ref[...] = value[j * per:(j + 1) * per, :]


def finish_kernel(*refs):
    out_ref = refs[-1]
    total = refs[0][...].astype(F32)
    for ref in refs[1:-1]:
        total += ref[...].astype(F32)
    total = total.astype(BF16)
    rows, lanes = total.shape
    count = out_ref.shape[0]
    row, col = iota((count, rows), 0), iota((count, rows), 1)
    for c in range(CHUNKS):
        pick = onehot(col == row * CHUNKS + c)
        out_ref[:, c * lanes:(c + 1) * lanes] = mm(pick, total).astype(BF16)


def call(kernel, out_shape, in_specs=None, scratch=(), limit=8 << 20, **kw):
    return pl.pallas_call(
        kernel,
        out_shape=out_shape,
        scratch_shapes=scratch,
        compiler_params=pltpu.CompilerParams(vmem_limit_bytes=limit),
        **({} if in_specs is None else {"in_specs": in_specs}),
        **kw,
    )


def in_hbm(x):
    return pltpu.with_memory_space_constraint(x, pltpu.HBM)


def fetch_kernel(*refs):
    sems = refs[-1]
    half = len(refs) // 2
    copies = [pltpu.make_async_copy(refs[i], refs[half + i], sems.at[i]) for i in range(half)]
    for copy in copies:
        copy.start()
    for copy in copies:
        copy.wait()


def fetch(*arrays):
    size = sum(a.size * 2 for a in arrays)
    return call(
        fetch_kernel,
        [jax.ShapeDtypeStruct(a.shape, a.dtype) for a in arrays],
        [pl.BlockSpec(memory_space=pltpu.HBM)] * len(arrays),
        (pltpu.SemaphoreType.DMA((len(arrays),)),),
        limit=16 << 20,
        cost_estimate=pl.CostEstimate(flops=0, bytes_accessed=2 * size, transcendentals=0),
    )(*map(in_hbm, arrays))


def body(tokens, expert_ids, gate_weights, placement, w_gate, w_up, w_down):
    n_expert, n_dp = lax.axis_size("expert"), lax.axis_size("dp")
    count, width = tokens.shape
    topk = expert_ids.shape[1]
    group = count * n_dp
    assert group <= LANES and n_expert < 256 and width % (CHUNKS * LANES) == 0
    assert width >= 2 * CHUNKS * LANES and placement.shape[1] <= 8
    first = max(2, group * topk // n_expert)
    slots = first + max(1, first // 2)
    lanes = width // CHUNKS
    per = count * CHUNKS
    extra = -(-2 * topk // 8) * 8
    total = n_expert * slots * CHUNKS
    shape = lambda *dims: jax.ShapeDtypeStruct(dims, BF16)
    hbm = pl.BlockSpec(memory_space=pltpu.HBM)
    big = total > 1024

    packed = call(
        pack_kernel,
        shape(per + extra, lanes),
        [hbm] * 4,
        (
            pltpu.VMEM((count, width), BF16),
            pltpu.VMEM((topk, count), I32),
            pltpu.VMEM((topk, count), BF16),
            pltpu.VMEM(placement.shape, I32),
            pltpu.SemaphoreType.DMA((4,)),
        ),
    )(*map(in_hbm, (tokens, expert_ids.T, gate_weights.T, placement)))
    weights = fetch(w_gate[0], w_up[0], w_down[0])
    blocks = [packed] + [swap(packed, "dp", j, n_dp) for j in range(1, n_dp)]
    hot = placement.shape[1]
    *sends, mix = call(
        functools.partial(select_kernel, n_expert, n_dp, first, slots, topk, hot),
        [shape(slots * CHUNKS, lanes)] * n_expert + [shape(total, n_dp * per)],
        scratch=(pltpu.VMEM((n_dp * per, lanes), BF16),),
        limit=40 << 20 if big else 8 << 20,
    )(*blocks)
    rows = [sends[0]] + [swap(sends[j], "expert", j, n_expert) for j in range(1, n_expert)]
    parts = call(
        functools.partial(expert_kernel, n_expert),
        [shape(slots * CHUNKS, lanes)] * n_expert,
        scratch=(
            pltpu.VMEM((total // CHUNKS, width), BF16),
            pltpu.VMEM((total, lanes), BF16),
        ),
        limit=60 << 20 if big else 24 << 20,
    )(*rows, *weights)
    backs = [parts[0]] + [swap(parts[j], "expert", j, n_expert) for j in range(1, n_expert)]
    outs = call(
        functools.partial(mix_kernel, n_expert),
        [shape(per, lanes)] * n_dp,
        scratch=(pltpu.VMEM((total, lanes), BF16),),
        limit=24 << 20 if big else 8 << 20,
    )(*backs, mix)
    pieces = [outs[0]] + [swap(outs[j], "dp", j, n_dp) for j in range(1, n_dp)]
    return call(finish_kernel, shape(count, width))(*pieces)


def solution(mesh):
    placed = (
        P(("groups", "expert", "dp"), None),
        P(("groups", "expert", "dp"), None),
        P(("groups", "expert", "dp"), None),
        P("groups", None),
        P("expert", "dp", None),
        P("expert", "dp", None),
        P("expert", "dp", None),
    )
    return jax.shard_map(
        body,
        mesh=mesh,
        in_specs=placed,
        out_specs=P(("groups", "expert", "dp"), None),
        check_vma=False,
    )
```

```python
import functools

import jax
import jax.numpy as jnp
from jax import lax
from jax.experimental import pallas as pl
from jax.experimental.pallas import tpu as pltpu
from jax.sharding import PartitionSpec as P

BF16, F32, I32 = jnp.bfloat16, jnp.float32, jnp.int32
CHUNKS = 8
LANES = 128


def iota(shape, dim):
    return lax.broadcasted_iota(I32, shape, dim)


def onehot(cond):
    return jnp.where(cond, 1.0, 0.0).astype(BF16)


def mm(a, b, contract=((1,), (0,))):
    return lax.dot_general(a, b, (contract, ((), ())), preferred_element_type=F32)


def dot(a, b, contract=((1,), (0,))):
    return mm(a.astype(BF16), b.astype(BF16), contract)


def partner(me, step, n):
    if n & (n - 1) == 0:
        return me ^ step
    return (step + n - me) % n


def swap(x, axis, step, n):
    return lax.ppermute(x, axis, [(i, partner(i, step, n)) for i in range(n)])


def swap_chips(x, step, n):
    return lax.ppermute(
        x, "expert", [(i, 2 * partner(i // 2, step, n // 2) + i % 2) for i in range(n)]
    )


def swap_cores(x, n):
    return lax.ppermute(x, "expert", [(i, i ^ 1) for i in range(n)])


def pack_kernel(tok_hbm, ids_hbm, gate_hbm, place_hbm, out_ref, tok_ref, ids_ref, gate_ref, place_ref, sems):
    pairs = ((ids_hbm, ids_ref), (gate_hbm, gate_ref), (place_hbm, place_ref), (tok_hbm, tok_ref))
    copies = [pltpu.make_async_copy(a, b, sems.at[i]) for i, (a, b) in enumerate(pairs)]
    for copy in copies:
        copy.start()
    count, width = tok_ref.shape
    topk = ids_ref.shape[0]
    lanes = width // CHUNKS
    rows = count * CHUNKS
    extra = out_ref.shape[0] - rows
    me = lax.axis_index("dp")
    place = onehot(iota((count, LANES), 1) == iota((count, LANES), 0) + me * count)
    ids_row = onehot(iota((extra, topk), 0) == iota((extra, topk), 1))
    gate_row = onehot(iota((extra, topk), 0) == iota((extra, topk), 1) + topk)
    for copy in copies[:3]:
        copy.wait()
    small = dot(ids_row, (ids_ref[...] + 1).astype(F32)) + dot(gate_row, gate_ref[...])
    out_ref[rows:, :LANES] = dot(small, place).astype(BF16)
    line = iota((extra, LANES), 0)
    listed = jnp.zeros((extra, LANES), F32)
    for h in range(place_ref.shape[1]):
        listed = jnp.where(line == h, (place_ref[0:1, h:h + 1] + 1).astype(F32), listed)
    out_ref[rows:, LANES:2 * LANES] = listed.astype(BF16)
    out_ref[rows:, 2 * LANES:] = jnp.zeros((extra, lanes - 2 * LANES), BF16)
    acc = jnp.zeros((rows, lanes), F32)
    row, col = iota((rows, count), 0), iota((rows, count), 1)
    copies[3].wait()
    for c in range(CHUNKS):
        pick = onehot(row == col * CHUNKS + c)
        acc += mm(pick, tok_ref[:, c * lanes:(c + 1) * lanes])
    out_ref[:rows, :] = acc.astype(BF16)


def select_kernel(n_expert, n_dp, first, slots, topk, hot, *refs):
    steps = n_expert // 2
    blocks, sends = refs[:2 * n_dp], refs[2 * n_dp:2 * n_dp + steps]
    mix_ref, group_ref = refs[2 * n_dp + steps:]
    per = group_ref.shape[0] // (2 * n_dp)
    count = per // CHUNKS
    half = slots * CHUNKS
    total = steps * 2 * half
    me, mine = lax.axis_index("dp"), lax.axis_index("expert")
    small = [None, None]
    for j, ref in enumerate(blocks):
        group_ref[j * per:(j + 1) * per, :] = ref[:per, :]
        part = ref[per:, :LANES].astype(F32)
        which = j // n_dp
        small[which] = part if small[which] is None else small[which] + part
    places = blocks[0][per:, LANES:2 * LANES].astype(F32)
    row = iota((total, LANES), 0)
    piece = row // half
    expert = (2 * partner(mine // 2, piece // 2, steps) + mine % 2).astype(F32)
    own = piece % 2 == 0
    slot = ((row - piece * half) // CHUNKS).astype(F32)
    named = jnp.zeros((total, LANES), F32)
    gate = jnp.zeros((total, LANES), F32)
    for k in range(topk):
        hit = jnp.where(own, small[0][k:k + 1, :], small[1][k:k + 1, :]) == expert + 1.0
        named = jnp.where(hit, 1.0, named)
        k += topk
        gate = jnp.where(hit, jnp.where(own, small[0][k:k + 1, :], small[1][k:k + 1, :]), gate)
    earlier = onehot(iota((LANES, LANES), 0) < iota((LANES, LANES), 1))
    rank = dot(named, earlier)
    allowed = slot < first
    for h in range(hot):
        allowed |= expert + 1.0 == places[h:h + 1, :]
    chosen = jnp.where(allowed & (rank == slot), named, 0.0)
    columns = 2 * n_dp * per
    at = iota((LANES, columns), 1) % (n_dp * per)
    token = partner(me, at // per, n_dp) * count + (at % per) // CHUNKS
    spread = onehot(iota((LANES, columns), 0) == token)
    row, col = iota((total, columns), 0), iota((total, columns), 1)
    same = (row % CHUNKS == col % CHUNKS) & ((row // half) % 2 == col // (n_dp * per))
    pick = jnp.where(same, dot(chosen, spread), 0.0).astype(BF16)
    value = mm(pick, group_ref[...]).astype(BF16)
    for j, ref in enumerate(sends):
        ref[...] = value[j * 2 * half:(j + 1) * 2 * half, :]
    mix_ref[...] = jnp.where(same, dot(chosen * gate, spread), 0.0).astype(BF16)


def expert_kernel(steps, *refs):
    ins, outs = refs[:steps], refs[steps + 4:2 * steps + 4]
    gate_ref, up_ref, down_ref, order_ref = refs[steps:steps + 4]
    x_ref, y_ref = refs[2 * steps + 4:]
    total, lanes = y_ref.shape
    piece = total // steps
    count = total // CHUNKS
    nt = ((1,), (1,))
    for j, ref in enumerate(ins):
        y_ref[j * piece:(j + 1) * piece, :] = ref[...]
    x = mm(order_ref[...], y_ref[...]).astype(BF16)
    for c in range(CHUNKS):
        x_ref[:, c * lanes:(c + 1) * lanes] = x[c * count:(c + 1) * count, :]
    gate = mm(x_ref[...], gate_ref[...], nt)
    up = mm(x_ref[...], up_ref[...], nt)
    hidden = (gate / (1.0 + jnp.exp(-gate)) * up).astype(BF16)
    for c in range(CHUNKS):
        value = mm(hidden, down_ref[:, c * lanes:(c + 1) * lanes]).astype(BF16)
        y_ref[c * count:(c + 1) * count, :] = value
    y = mm(order_ref[...], y_ref[...], ((0,), (0,))).astype(BF16)
    for j, ref in enumerate(outs):
        ref[...] = y[j * piece:(j + 1) * piece, :]


def mix_kernel(steps, *refs):
    backs, mix_ref = refs[:steps], refs[steps]
    own_ref, other_ref, rows_ref = refs[steps + 1:]
    piece = backs[0].shape[0]
    for j, ref in enumerate(backs):
        rows_ref[j * piece:(j + 1) * piece, :] = ref[...]
    value = mm(mix_ref[...], rows_ref[...], ((0,), (0,)))
    half = own_ref.shape[0]
    own_ref[...] = value[:half, :]
    other_ref[...] = value[half:, :]


def join_kernel(own_ref, other_ref, *out_refs):
    value = (own_ref[...] + other_ref[...]).astype(BF16)
    per = out_refs[0].shape[0]
    for j, ref in enumerate(out_refs):
        ref[...] = value[j * per:(j + 1) * per, :]


def finish_kernel(*refs):
    out_ref = refs[-1]
    total = refs[0][...].astype(F32)
    for ref in refs[1:-1]:
        total += ref[...].astype(F32)
    total = total.astype(BF16)
    rows, lanes = total.shape
    count = out_ref.shape[0]
    row, col = iota((count, rows), 0), iota((count, rows), 1)
    for c in range(CHUNKS):
        pick = onehot(col == row * CHUNKS + c)
        out_ref[:, c * lanes:(c + 1) * lanes] = mm(pick, total).astype(BF16)


def call(kernel, out_shape, in_specs=None, scratch=(), limit=8 << 20, **kw):
    return pl.pallas_call(
        kernel,
        out_shape=out_shape,
        scratch_shapes=scratch,
        compiler_params=pltpu.CompilerParams(vmem_limit_bytes=limit),
        **({} if in_specs is None else {"in_specs": in_specs}),
        **kw,
    )


def in_hbm(x):
    return pltpu.with_memory_space_constraint(x, pltpu.HBM)


def fetch_kernel(*refs):
    order_ref, sems = refs[-2:]
    half = len(refs) // 2 - 1
    copies = [pltpu.make_async_copy(refs[i], refs[half + i], sems.at[i]) for i in range(half)]
    for copy in copies:
        copy.start()
    total = order_ref.shape[0]
    count = total // CHUNKS
    row, col = iota((total, total), 0), iota((total, total), 1)
    order_ref[...] = onehot(col == (row % count) * CHUNKS + row // count)
    for copy in copies:
        copy.wait()


def fetch(total, limit, *arrays):
    size = sum(a.size * 2 for a in arrays)
    return call(
        fetch_kernel,
        [jax.ShapeDtypeStruct(a.shape, a.dtype) for a in arrays]
        + [jax.ShapeDtypeStruct((total, total), BF16)],
        [pl.BlockSpec(memory_space=pltpu.HBM)] * len(arrays),
        (pltpu.SemaphoreType.DMA((len(arrays),)),),
        limit=limit,
        cost_estimate=pl.CostEstimate(flops=0, bytes_accessed=2 * size, transcendentals=0),
    )(*map(in_hbm, arrays))


def body(tokens, expert_ids, gate_weights, placement, w_gate, w_up, w_down):
    n_expert, n_dp = lax.axis_size("expert"), lax.axis_size("dp")
    count, width = tokens.shape
    topk = expert_ids.shape[1]
    group = count * n_dp
    assert n_expert % 2 == 0 and group <= LANES and n_expert < 256 and width % (CHUNKS * LANES) == 0
    assert width >= 2 * CHUNKS * LANES and placement.shape[1] <= 8
    first = max(2, group * topk // n_expert)
    slots = first + max(1, first // 2)
    lanes = width // CHUNKS
    per = count * CHUNKS
    extra = -(-2 * topk // 8) * 8
    total = n_expert * slots * CHUNKS
    shape = lambda *dims: jax.ShapeDtypeStruct(dims, BF16)
    hbm = pl.BlockSpec(memory_space=pltpu.HBM)
    big = total > 1024

    packed = call(
        pack_kernel,
        shape(per + extra, lanes),
        [hbm] * 4,
        (
            pltpu.VMEM((count, width), BF16),
            pltpu.VMEM((topk, count), I32),
            pltpu.VMEM((topk, count), BF16),
            pltpu.VMEM(placement.shape, I32),
            pltpu.SemaphoreType.DMA((4,)),
        ),
    )(*map(in_hbm, (tokens, expert_ids.T, gate_weights.T, placement)))
    steps = n_expert // 2
    weights = fetch(total, 48 << 20 if big else 16 << 20, w_gate[0], w_up[0], w_down[0])
    blocks = [packed] + [swap(packed, "dp", j, n_dp) for j in range(1, n_dp)]
    blocks += [swap_cores(block, n_expert) for block in blocks]
    hot = placement.shape[1]
    *sends, mix = call(
        functools.partial(select_kernel, n_expert, n_dp, first, slots, topk, hot),
        [shape(2 * slots * CHUNKS, lanes)] * steps + [shape(total, 2 * n_dp * per)],
        scratch=(pltpu.VMEM((2 * n_dp * per, lanes), BF16),),
        limit=48 << 20 if big else 8 << 20,
    )(*blocks)
    rows = [sends[0]] + [swap_chips(sends[j], j, n_expert) for j in range(1, steps)]
    parts = call(
        functools.partial(expert_kernel, steps),
        [shape(2 * slots * CHUNKS, lanes)] * steps,
        scratch=(
            pltpu.VMEM((total // CHUNKS, width), BF16),
            pltpu.VMEM((total, lanes), BF16),
        ),
        limit=60 << 20 if big else 24 << 20,
    )(*rows, *weights)
    backs = [parts[0]] + [swap_chips(parts[j], j, n_expert) for j in range(1, steps)]
    own, other = call(
        functools.partial(mix_kernel, steps),
        [jax.ShapeDtypeStruct((n_dp * per, lanes), F32)] * 2,
        scratch=(pltpu.VMEM((total, lanes), BF16),),
        limit=32 << 20 if big else 8 << 20,
    )(*backs, mix)
    outs = call(join_kernel, [shape(per, lanes)] * n_dp)(own, swap_cores(other, n_expert))
    pieces = [outs[0]] + [swap(outs[j], "dp", j, n_dp) for j in range(1, n_dp)]
    return call(finish_kernel, shape(count, width))(*pieces)


def solution(mesh):
    placed = (
        P(("groups", "expert", "dp"), None),
        P(("groups", "expert", "dp"), None),
        P(("groups", "expert", "dp"), None),
        P("groups", None),
        P("expert", "dp", None),
        P("expert", "dp", None),
        P("expert", "dp", None),
    )
    return jax.shard_map(
        body,
        mesh=mesh,
        in_specs=placed,
        out_specs=P(("groups", "expert", "dp"), None),
        check_vma=False,
    )
```

```python
import functools

import jax
import jax.numpy as jnp
from jax import lax
from jax.experimental import pallas as pl
from jax.experimental.pallas import tpu as pltpu
from jax.sharding import PartitionSpec as P


BF16, F32, I32 = jnp.bfloat16, jnp.float32, jnp.int32
CHUNKS = 8
LANES = 128


def iota(shape, dim):
    return lax.broadcasted_iota(I32, shape, dim)


def onehot(cond):
    return jnp.where(cond, 1.0, 0.0).astype(BF16)


def mm(a, b, contract=((1,), (0,))):
    return lax.dot_general(a, b, (contract, ((), ())), preferred_element_type=F32)


def dot(a, b, contract=((1,), (0,))):
    return mm(a.astype(BF16), b.astype(BF16), contract)


def partner(me, step, n):
    if n & (n - 1) == 0:
        return me ^ step
    return (step + n - me) % n


def swap(xs, n):
    out = [xs[0]]
    for j in range(1, n):
        out.append(lax.ppermute(xs[j], "dp", [(i, partner(i, j, n)) for i in range(n)]))
    return out


def swap_chips(xs, n):
    out = [xs[0]]
    for j in range(1, n // 2):
        pairs = [(i, 2 * partner(i // 2, j, n // 2) + i % 2) for i in range(n)]
        out.append(lax.ppermute(xs[j], "expert", pairs))
    return out


def swap_cores(x, n):
    return lax.ppermute(x, "expert", [(i, i ^ 1) for i in range(n)])


def pack_kernel(tok_hbm, ids_hbm, gate_hbm, place_hbm, out_ref, tok_ref, ids_ref, gate_ref, place_ref, sems):
    pairs = ((ids_hbm, ids_ref), (gate_hbm, gate_ref), (place_hbm, place_ref), (tok_hbm, tok_ref))
    copies = [pltpu.make_async_copy(a, b, sems.at[i]) for i, (a, b) in enumerate(pairs)]
    for copy in copies:
        copy.start()
    count, width = tok_ref.shape
    topk = ids_ref.shape[0]
    lanes = width // CHUNKS
    rows = count * CHUNKS
    extra = out_ref.shape[0] - rows
    me = lax.axis_index("dp")
    place = onehot(iota((count, LANES), 1) == iota((count, LANES), 0) + me * count)
    ids_row = onehot(iota((extra, topk), 0) == iota((extra, topk), 1))
    gate_row = onehot(iota((extra, topk), 0) == iota((extra, topk), 1) + topk)
    for copy in copies[:3]:
        copy.wait()
    small = dot(ids_row, (ids_ref[...] + 1).astype(F32)) + dot(gate_row, gate_ref[...])
    out_ref[rows:, :LANES] = dot(small, place).astype(BF16)
    line = iota((extra, LANES), 0)
    listed = jnp.zeros((extra, LANES), F32)
    for h in range(place_ref.shape[1]):
        listed = jnp.where(line == h, (place_ref[0:1, h:h + 1] + 1).astype(F32), listed)
    out_ref[rows:, LANES:2 * LANES] = listed.astype(BF16)
    out_ref[rows:, 2 * LANES:] = jnp.zeros((extra, lanes - 2 * LANES), BF16)
    acc = jnp.zeros((rows, lanes), F32)
    row, col = iota((rows, count), 0), iota((rows, count), 1)
    copies[3].wait()
    for c in range(CHUNKS):
        pick = onehot(row == col * CHUNKS + c)
        acc += mm(pick, tok_ref[:, c * lanes:(c + 1) * lanes])
    out_ref[:rows, :] = acc.astype(BF16)


def select_kernel(n_expert, n_dp, first, slots, topk, hot, *refs):
    steps = n_expert // 2
    blocks, sends = refs[:2 * n_dp], refs[2 * n_dp:2 * n_dp + steps]
    mix_ref, group_ref = refs[2 * n_dp + steps:]
    per = group_ref.shape[0] // (2 * n_dp)
    count = per // CHUNKS
    half = slots * CHUNKS
    total = steps * 2 * half
    me, mine = lax.axis_index("dp"), lax.axis_index("expert")
    small = [None, None]
    for j, ref in enumerate(blocks):
        group_ref[j * per:(j + 1) * per, :] = ref[:per, :]
        part = ref[per:, :LANES].astype(F32)
        which = j // n_dp
        small[which] = part if small[which] is None else small[which] + part
    places = blocks[0][per:, LANES:2 * LANES].astype(F32)
    row = iota((total, LANES), 0)
    piece = row // half
    expert = (2 * partner(mine // 2, piece // 2, steps) + mine % 2).astype(F32)
    own = piece % 2 == 0
    slot = ((row - piece * half) // CHUNKS).astype(F32)
    named = jnp.zeros((total, LANES), F32)
    gate = jnp.zeros((total, LANES), F32)
    for k in range(topk):
        hit = jnp.where(own, small[0][k:k + 1, :], small[1][k:k + 1, :]) == expert + 1.0
        named = jnp.where(hit, 1.0, named)
        k += topk
        gate = jnp.where(hit, jnp.where(own, small[0][k:k + 1, :], small[1][k:k + 1, :]), gate)
    earlier = onehot(iota((LANES, LANES), 0) < iota((LANES, LANES), 1))
    rank = dot(named, earlier)
    allowed = slot < first
    for h in range(hot):
        allowed |= expert + 1.0 == places[h:h + 1, :]
    chosen = jnp.where(allowed & (rank == slot), named, 0.0)
    columns = 2 * n_dp * per
    at = iota((LANES, columns), 1) % (n_dp * per)
    token = partner(me, at // per, n_dp) * count + (at % per) // CHUNKS
    spread = onehot(iota((LANES, columns), 0) == token)
    row, col = iota((total, columns), 0), iota((total, columns), 1)
    same = (row % CHUNKS == col % CHUNKS) & ((row // half) % 2 == col // (n_dp * per))
    pick = jnp.where(same, dot(chosen, spread), 0.0).astype(BF16)
    value = mm(pick, group_ref[...]).astype(BF16)
    for j, ref in enumerate(sends):
        ref[...] = value[j * 2 * half:(j + 1) * 2 * half, :]
    mix_ref[...] = jnp.where(same, dot(chosen * gate, spread), 0.0).astype(BF16)


def expert_kernel(steps, *refs):
    ins, outs = refs[:steps], refs[steps + 4:2 * steps + 4]
    gate_ref, up_ref, down_ref, order_ref = refs[steps:steps + 4]
    x_ref, y_ref = refs[2 * steps + 4:]
    total, lanes = y_ref.shape
    piece = total // steps
    count = total // CHUNKS
    nt = ((1,), (1,))
    for j, ref in enumerate(ins):
        y_ref[j * piece:(j + 1) * piece, :] = ref[...]
    x = mm(order_ref[...], y_ref[...]).astype(BF16)
    for c in range(CHUNKS):
        x_ref[:, c * lanes:(c + 1) * lanes] = x[c * count:(c + 1) * count, :]
    gate = mm(x_ref[...], gate_ref[...], nt)
    up = mm(x_ref[...], up_ref[...], nt)
    hidden = (gate / (1.0 + jnp.exp(-gate)) * up).astype(BF16)
    for c in range(CHUNKS):
        value = mm(hidden, down_ref[:, c * lanes:(c + 1) * lanes]).astype(BF16)
        y_ref[c * count:(c + 1) * count, :] = value
    y = mm(order_ref[...], y_ref[...], ((0,), (0,))).astype(BF16)
    for j, ref in enumerate(outs):
        ref[...] = y[j * piece:(j + 1) * piece, :]


def mix_kernel(steps, *refs):
    backs, mix_ref = refs[:steps], refs[steps]
    own_ref, other_ref, rows_ref = refs[steps + 1:]
    piece = backs[0].shape[0]
    for j, ref in enumerate(backs):
        rows_ref[j * piece:(j + 1) * piece, :] = ref[...]
    value = mm(mix_ref[...], rows_ref[...], ((0,), (0,)))
    half = own_ref.shape[0]
    own_ref[...] = value[:half, :]
    other_ref[...] = value[half:, :]


def join_kernel(own_ref, other_ref, *out_refs):
    value = (own_ref[...] + other_ref[...]).astype(BF16)
    per = out_refs[0].shape[0]
    for j, ref in enumerate(out_refs):
        ref[...] = value[j * per:(j + 1) * per, :]


def finish_kernel(*refs):
    out_ref = refs[-1]
    total = refs[0][...].astype(F32)
    for ref in refs[1:-1]:
        total += ref[...].astype(F32)
    total = total.astype(BF16)
    rows, lanes = total.shape
    count = out_ref.shape[0]
    row, col = iota((count, rows), 0), iota((count, rows), 1)
    for c in range(CHUNKS):
        pick = onehot(col == row * CHUNKS + c)
        out_ref[:, c * lanes:(c + 1) * lanes] = mm(pick, total).astype(BF16)


def call(kernel, out_shape, in_specs=None, scratch=(), limit=8 << 20, **kw):
    return pl.pallas_call(
        kernel,
        out_shape=out_shape,
        scratch_shapes=scratch,
        compiler_params=pltpu.CompilerParams(vmem_limit_bytes=limit),
        **({} if in_specs is None else {"in_specs": in_specs}),
        **kw,
    )


def in_hbm(x):
    return pltpu.with_memory_space_constraint(x, pltpu.HBM)


def fetch_kernel(*refs):
    order_ref, sems = refs[-2:]
    half = len(refs) // 2 - 1
    copies = [pltpu.make_async_copy(refs[i], refs[half + i], sems.at[i]) for i in range(half)]
    for copy in copies:
        copy.start()
    total = order_ref.shape[0]
    count = total // CHUNKS
    row, col = iota((total, total), 0), iota((total, total), 1)
    order_ref[...] = onehot(col == (row % count) * CHUNKS + row // count)
    for copy in copies:
        copy.wait()


def fetch(total, limit, *arrays):
    size = sum(a.size * 2 for a in arrays)
    return call(
        fetch_kernel,
        [jax.ShapeDtypeStruct(a.shape, a.dtype) for a in arrays]
        + [jax.ShapeDtypeStruct((total, total), BF16)],
        [pl.BlockSpec(memory_space=pltpu.HBM)] * len(arrays),
        (pltpu.SemaphoreType.DMA((len(arrays),)),),
        limit=limit,
        cost_estimate=pl.CostEstimate(flops=0, bytes_accessed=2 * size, transcendentals=0),
    )(*map(in_hbm, arrays))


def body(tokens, expert_ids, gate_weights, placement, w_gate, w_up, w_down):
    n_expert, n_dp = lax.axis_size("expert"), lax.axis_size("dp")
    count, width = tokens.shape
    topk = expert_ids.shape[1]
    group = count * n_dp
    assert n_expert % 2 == 0 and group <= LANES and n_expert < 256 and width % (CHUNKS * LANES) == 0
    assert width >= 2 * CHUNKS * LANES and placement.shape[1] <= 8
    first = max(2, group * topk // n_expert)
    slots = first + max(1, first // 2)
    lanes = width // CHUNKS
    per = count * CHUNKS
    extra = -(-2 * topk // 8) * 8
    total = n_expert * slots * CHUNKS
    shape = lambda *dims: jax.ShapeDtypeStruct(dims, BF16)
    hbm = pl.BlockSpec(memory_space=pltpu.HBM)
    big = total > 1024

    packed = call(
        pack_kernel,
        shape(per + extra, lanes),
        [hbm] * 4,
        (
            pltpu.VMEM((count, width), BF16),
            pltpu.VMEM((topk, count), I32),
            pltpu.VMEM((topk, count), BF16),
            pltpu.VMEM(placement.shape, I32),
            pltpu.SemaphoreType.DMA((4,)),
        ),
    )(*map(in_hbm, (tokens, expert_ids.T, gate_weights.T, placement)))
    steps = n_expert // 2
    weights = fetch(total, 48 << 20 if big else 16 << 20, w_gate[0], w_up[0], w_down[0])
    blocks = swap([packed] * n_dp, n_dp)
    blocks += [swap_cores(block, n_expert) for block in blocks]
    hot = placement.shape[1]
    *sends, mix = call(
        functools.partial(select_kernel, n_expert, n_dp, first, slots, topk, hot),
        [shape(2 * slots * CHUNKS, lanes)] * steps + [shape(total, 2 * n_dp * per)],
        scratch=(pltpu.VMEM((2 * n_dp * per, lanes), BF16),),
        limit=48 << 20 if big else 8 << 20,
    )(*blocks)
    rows = swap_chips(sends, n_expert)
    parts = call(
        functools.partial(expert_kernel, steps),
        [shape(2 * slots * CHUNKS, lanes)] * steps,
        scratch=(
            pltpu.VMEM((total // CHUNKS, width), BF16),
            pltpu.VMEM((total, lanes), BF16),
        ),
        limit=60 << 20 if big else 24 << 20,
    )(*rows, *weights)
    backs = swap_chips(parts, n_expert)
    own, other = call(
        functools.partial(mix_kernel, steps),
        [jax.ShapeDtypeStruct((n_dp * per, lanes), F32)] * 2,
        scratch=(pltpu.VMEM((total, lanes), BF16),),
        limit=32 << 20 if big else 8 << 20,
    )(*backs, mix)
    outs = call(join_kernel, [shape(per, lanes)] * n_dp)(own, swap_cores(other, n_expert))
    pieces = swap(outs, n_dp)
    return call(finish_kernel, shape(count, width))(*pieces)


def solution(mesh):
    placed = (
        P(("groups", "expert", "dp"), None),
        P(("groups", "expert", "dp"), None),
        P(("groups", "expert", "dp"), None),
        P("groups", None),
        P("expert", "dp", None),
        P("expert", "dp", None),
        P("expert", "dp", None),
    )
    return jax.shard_map(
        body,
        mesh=mesh,
        in_specs=placed,
        out_specs=P(("groups", "expert", "dp"), None),
        check_vma=False,
    )
```

```python
import functools

import jax
import jax.numpy as jnp
from jax import lax
from jax.experimental import pallas as pl
from jax.experimental.pallas import tpu as pltpu
from jax.sharding import PartitionSpec as P


BF16, F32, I32 = jnp.bfloat16, jnp.float32, jnp.int32
CHUNKS = 8
LANES = 128


def iota(shape, dim):
    return lax.broadcasted_iota(I32, shape, dim)


def onehot(cond):
    return jnp.where(cond, 1.0, 0.0).astype(BF16)


def mm(a, b, contract=((1,), (0,))):
    return lax.dot_general(a, b, (contract, ((), ())), preferred_element_type=F32)


def dot(a, b, contract=((1,), (0,))):
    return mm(a.astype(BF16), b.astype(BF16), contract)


def partner(me, step, n):
    if n & (n - 1) == 0:
        return me ^ step
    return (step + n - me) % n


def swap(xs, axis):
    n = len(xs)
    out = [xs[0]]
    for j in range(1, n):
        out.append(lax.ppermute(xs[j], axis, [(i, partner(i, j, n)) for i in range(n)]))
    return out


def pack_kernel(tok_hbm, ids_hbm, gate_hbm, place_hbm, *refs):
    out_ref, spread_ref, earlier_ref, tok_ref, ids_ref, gate_ref, place_ref, sems = refs
    pairs = ((ids_hbm, ids_ref), (gate_hbm, gate_ref), (place_hbm, place_ref), (tok_hbm, tok_ref))
    copies = [pltpu.make_async_copy(a, b, sems.at[i]) for i, (a, b) in enumerate(pairs)]
    for copy in copies:
        copy.start()
    count, width = tok_ref.shape
    topk = ids_ref.shape[0]
    lanes = width // CHUNKS
    rows = count * CHUNKS
    extra = out_ref.shape[0] - rows
    me = lax.axis_index("dp")
    columns = spread_ref.shape[1]
    at = iota((LANES, columns), 1)
    token = partner(me, at // rows, columns // rows) * count + at % count
    spread_ref[...] = onehot(iota((LANES, columns), 0) == token)
    earlier_ref[...] = onehot(iota((LANES, columns), 0) < token)
    place = onehot(iota((count, LANES), 1) == iota((count, LANES), 0) + me * count)
    ids_row = onehot(iota((extra, topk), 0) == iota((extra, topk), 1))
    gate_row = onehot(iota((extra, topk), 0) == iota((extra, topk), 1) + topk)
    out_ref[rows:, 2 * LANES:] = jnp.zeros((extra, lanes - 2 * LANES), BF16)
    for copy in copies:
        copy.wait()
    for c in range(CHUNKS):
        out_ref[c * count:(c + 1) * count, :] = tok_ref[:, c * lanes:(c + 1) * lanes]
    small = dot(ids_row, (ids_ref[...] + 1).astype(F32)) + dot(gate_row, gate_ref[...])
    out_ref[rows:, :LANES] = dot(small, place).astype(BF16)
    line = iota((extra, LANES), 0)
    listed = jnp.zeros((extra, LANES), F32)
    for h in range(place_ref.shape[1]):
        listed = jnp.where(line == h, (place_ref[0:1, h:h + 1] + 1).astype(F32), listed)
    out_ref[rows:, LANES:2 * LANES] = listed.astype(BF16)


def row_experts(total, columns, piece, n_expert):
    step = iota((total, columns), 0) // piece
    return step, partner(lax.axis_index("expert"), step, n_expert).astype(F32) + 1.0


def select_kernel(n_expert, n_dp, first, slots, topk, hot, *refs):
    blocks, spread_ref, earlier_ref = refs[:n_dp], refs[n_dp], refs[n_dp + 1]
    sends = refs[n_dp + 2:n_dp + 2 + n_expert]
    pick_ref, small_ref, group_ref = refs[n_dp + 2 + n_expert:]
    per = group_ref.shape[0] // n_dp
    count = per // CHUNKS
    piece = slots * CHUNKS
    total = n_expert * piece
    columns = n_dp * per
    small = None
    for j, ref in enumerate(blocks):
        group_ref[j * per:(j + 1) * per, :] = ref[:per, :]
        part = ref[per:, :LANES].astype(F32)
        small = part if small is None else small + part
    places = blocks[0][per:, LANES:2 * LANES].astype(F32)
    _, expert = row_experts(total, LANES, piece, n_expert)
    named = jnp.zeros((total, LANES), F32)
    for k in range(topk):
        named = jnp.where(small[k:k + 1, :] == expert, 1.0, named)
    rank = dot(named, earlier_ref[...])
    spread = dot(small, spread_ref[...])
    small_ref[...] = spread
    step, expert = row_experts(total, columns, piece, n_expert)
    row, col = iota((total, columns), 0), iota((total, columns), 1)
    slot = ((row - step * piece) // CHUNKS).astype(F32)
    allowed = slot < first
    for h in range(hot):
        allowed |= expert == places[h:h + 1, :1]
    hit = None
    for k in range(topk):
        same = spread[k:k + 1, :] == expert
        hit = same if hit is None else hit | same
    chunk = row % CHUNKS == (col % per) // count
    pick = onehot(hit & allowed & chunk & (rank == slot))
    pick_ref[...] = pick
    value = mm(pick, group_ref[...]).astype(BF16)
    for j, ref in enumerate(sends):
        ref[...] = value[j * piece:(j + 1) * piece, :]


def expert_kernel(steps, *refs):
    ins, outs = refs[:steps], refs[steps + 4:2 * steps + 4]
    gate_ref, up_ref, down_ref, order_ref = refs[steps:steps + 4]
    x_ref, y_ref = refs[2 * steps + 4:]
    total, lanes = y_ref.shape
    piece = total // steps
    count = total // CHUNKS
    nt = ((1,), (1,))
    for j, ref in enumerate(ins):
        y_ref[j * piece:(j + 1) * piece, :] = ref[...]
    x = mm(order_ref[...], y_ref[...]).astype(BF16)
    for c in range(CHUNKS):
        x_ref[:, c * lanes:(c + 1) * lanes] = x[c * count:(c + 1) * count, :]
    gate = mm(x_ref[...], gate_ref[...], nt)
    up = mm(x_ref[...], up_ref[...], nt)
    hidden = (gate / (1.0 + jnp.exp(-gate)) * up).astype(BF16)
    for c in range(CHUNKS):
        value = mm(hidden, down_ref[:, c * lanes:(c + 1) * lanes]).astype(BF16)
        y_ref[c * count:(c + 1) * count, :] = value
    y = mm(order_ref[...], y_ref[...], ((0,), (0,))).astype(BF16)
    for j, ref in enumerate(outs):
        ref[...] = y[j * piece:(j + 1) * piece, :]


def mix_kernel(steps, *refs):
    backs, mix_ref, out_refs, rows_ref = refs[:steps], refs[steps], refs[steps + 1:-1], refs[-1]
    piece = backs[0].shape[0]
    for j, ref in enumerate(backs):
        rows_ref[j * piece:(j + 1) * piece, :] = ref[...]
    value = mm(mix_ref[...], rows_ref[...], ((0,), (0,))).astype(BF16)
    per = out_refs[0].shape[0]
    for j, ref in enumerate(out_refs):
        ref[...] = value[j * per:(j + 1) * per, :]


def finish_kernel(*refs):
    out_ref = refs[-1]
    total = refs[0][...].astype(F32)
    for ref in refs[1:-1]:
        total += ref[...].astype(F32)
    total = total.astype(BF16)
    lanes = total.shape[1]
    count = out_ref.shape[0]
    for c in range(CHUNKS):
        out_ref[:, c * lanes:(c + 1) * lanes] = total[c * count:(c + 1) * count, :]


def call(kernel, out_shape, in_specs=None, scratch=(), limit=8 << 20, **kw):
    return pl.pallas_call(
        kernel,
        out_shape=out_shape,
        scratch_shapes=scratch,
        compiler_params=pltpu.CompilerParams(vmem_limit_bytes=limit),
        **({} if in_specs is None else {"in_specs": in_specs}),
        **kw,
    )


def in_hbm(x):
    return pltpu.with_memory_space_constraint(x, pltpu.HBM)


def fetch_kernel(n_expert, topk, *refs):
    ins, pick_ref, small_ref, outs, order_ref, mix_ref, sems = (
        refs[:3], refs[3], refs[4], refs[5:8], refs[8], refs[9], refs[10]
    )
    copies = [pltpu.make_async_copy(a, b, sems.at[i]) for i, (a, b) in enumerate(zip(ins, outs))]
    for copy in copies:
        copy.start()
    total, columns = pick_ref.shape
    count = total // CHUNKS
    row, col = iota((total, total), 0), iota((total, total), 1)
    order_ref[...] = onehot(col == (row % count) * CHUNKS + row // count)
    _, expert = row_experts(total, columns, total // n_expert, n_expert)
    gate = jnp.zeros((total, columns), F32)
    for k in range(topk):
        hit = small_ref[k:k + 1, :] == expert
        gate = jnp.where(hit, small_ref[topk + k:topk + k + 1, :], gate)
    mix_ref[...] = jnp.where(pick_ref[...].astype(F32) > 0.0, gate, 0.0).astype(BF16)
    for copy in copies:
        copy.wait()


def body(tokens, expert_ids, gate_weights, placement, w_gate, w_up, w_down):
    n_expert, n_dp = lax.axis_size("expert"), lax.axis_size("dp")
    count, width = tokens.shape
    topk = expert_ids.shape[1]
    group = count * n_dp
    assert group <= LANES and n_expert < 256 and width % (CHUNKS * LANES) == 0
    assert width >= 2 * CHUNKS * LANES and placement.shape[1] <= 8
    first = max(2, group * topk // n_expert)
    slots = first + max(1, first // 2)
    lanes = width // CHUNKS
    per = count * CHUNKS
    extra = -(-2 * topk // 8) * 8
    total = n_expert * slots * CHUNKS
    shape = lambda *dims: jax.ShapeDtypeStruct(dims, BF16)
    hbm = pl.BlockSpec(memory_space=pltpu.HBM)
    big = total > 1024

    columns = n_dp * per
    table = shape(LANES, columns)
    packed, spread, earlier = call(
        pack_kernel,
        [shape(per + extra, lanes), table, table],
        [hbm] * 4,
        (
            pltpu.VMEM((count, width), BF16),
            pltpu.VMEM((topk, count), I32),
            pltpu.VMEM((topk, count), BF16),
            pltpu.VMEM(placement.shape, I32),
            pltpu.SemaphoreType.DMA((4,)),
        ),
    )(*map(in_hbm, (tokens, expert_ids.T, gate_weights.T, placement)))
    blocks = swap([packed] * n_dp, "dp")
    hot = placement.shape[1]
    *sends, pick, small = call(
        functools.partial(select_kernel, n_expert, n_dp, first, slots, topk, hot),
        [shape(slots * CHUNKS, lanes)] * n_expert
        + [shape(total, columns), jax.ShapeDtypeStruct((extra, columns), F32)],
        scratch=(pltpu.VMEM((columns, lanes), BF16),),
        limit=48 << 20 if big else 8 << 20,
    )(*blocks, spread, earlier)
    weights = [w[0] for w in (w_gate, w_up, w_down)]
    vmem = pl.BlockSpec(memory_space=pltpu.VMEM)
    *weights, order, mix = call(
        functools.partial(fetch_kernel, n_expert, topk),
        [shape(*w.shape) for w in weights] + [shape(total, total), shape(total, columns)],
        [hbm] * 3 + [vmem] * 2,
        (pltpu.SemaphoreType.DMA((3,)),),
        limit=48 << 20 if big else 16 << 20,
        cost_estimate=pl.CostEstimate(
            flops=0, bytes_accessed=sum(4 * w.size for w in weights), transcendentals=0
        ),
    )(*map(in_hbm, weights), pick, small)
    rows = swap(sends, "expert")
    parts = call(
        functools.partial(expert_kernel, n_expert),
        [shape(slots * CHUNKS, lanes)] * n_expert,
        scratch=(
            pltpu.VMEM((total // CHUNKS, width), BF16),
            pltpu.VMEM((total, lanes), BF16),
        ),
        limit=60 << 20 if big else 24 << 20,
    )(*rows, *weights, order)
    backs = swap(parts, "expert")
    outs = call(
        functools.partial(mix_kernel, n_expert),
        [shape(per, lanes)] * n_dp,
        scratch=(pltpu.VMEM((total, lanes), BF16),),
        limit=32 << 20 if big else 8 << 20,
    )(*backs, mix)
    pieces = swap(outs, "dp")
    return call(finish_kernel, shape(count, width))(*pieces)


def solution(mesh):
    placed = (
        P(("groups", "expert", "dp"), None),
        P(("groups", "expert", "dp"), None),
        P(("groups", "expert", "dp"), None),
        P("groups", None),
        P("expert", "dp", None),
        P("expert", "dp", None),
        P("expert", "dp", None),
    )
    return jax.shard_map(
        body,
        mesh=mesh,
        in_specs=placed,
        out_specs=P(("groups", "expert", "dp"), None),
        check_vma=False,
    )
```

```python
import functools

import jax
import jax.numpy as jnp
from jax import lax
from jax.experimental import pallas as pl
from jax.experimental.pallas import tpu as pltpu
from jax.sharding import PartitionSpec as P


BF16, F32, I32 = jnp.bfloat16, jnp.float32, jnp.int32
CHUNKS = 8
LANES = 128
PARTS = 4


def iota(shape, dim):
    return lax.broadcasted_iota(I32, shape, dim)


def onehot(cond):
    return jnp.where(cond, 1.0, 0.0).astype(BF16)


def mm(a, b, contract=((1,), (0,))):
    return lax.dot_general(a, b, (contract, ((), ())), preferred_element_type=F32)


def dot(a, b, contract=((1,), (0,))):
    return mm(a.astype(BF16), b.astype(BF16), contract)


def partner(me, step, n):
    if n & (n - 1) == 0:
        return me ^ step
    return (step + n - me) % n


def swap(xs, axis):
    n = len(xs)
    out = [xs[0]]
    for j in range(1, n):
        out.append(lax.ppermute(xs[j], axis, [(i, partner(i, j, n)) for i in range(n)]))
    return out


def pack_kernel(tok_hbm, ids_hbm, gate_hbm, place_hbm, *refs):
    out_ref, spread_ref, earlier_ref, tok_ref, ids_ref, gate_ref, place_ref, sems = refs
    pairs = ((ids_hbm, ids_ref), (gate_hbm, gate_ref), (place_hbm, place_ref), (tok_hbm, tok_ref))
    copies = [pltpu.make_async_copy(a, b, sems.at[i]) for i, (a, b) in enumerate(pairs)]
    for copy in copies:
        copy.start()
    count, width = tok_ref.shape
    topk = ids_ref.shape[0]
    lanes = width // CHUNKS
    rows = count * CHUNKS
    extra = out_ref.shape[0] - rows
    me = lax.axis_index("dp")
    columns = spread_ref.shape[1]
    at = iota((LANES, columns), 1)
    token = partner(me, at // rows, columns // rows) * count + at % count
    spread_ref[...] = onehot(iota((LANES, columns), 0) == token)
    earlier_ref[...] = onehot(iota((LANES, columns), 0) < token)
    place = onehot(iota((count, LANES), 1) == iota((count, LANES), 0) + me * count)
    ids_row = onehot(iota((extra, topk), 0) == iota((extra, topk), 1))
    gate_row = onehot(iota((extra, topk), 0) == iota((extra, topk), 1) + topk)
    out_ref[rows:, 2 * LANES:] = jnp.zeros((extra, lanes - 2 * LANES), BF16)
    for copy in copies:
        copy.wait()
    for c in range(CHUNKS):
        out_ref[c * count:(c + 1) * count, :] = tok_ref[:, c * lanes:(c + 1) * lanes]
    small = dot(ids_row, (ids_ref[...] + 1).astype(F32)) + dot(gate_row, gate_ref[...])
    out_ref[rows:, :LANES] = dot(small, place).astype(BF16)
    line = iota((extra, LANES), 0)
    listed = jnp.zeros((extra, LANES), F32)
    for h in range(place_ref.shape[1]):
        listed = jnp.where(line == h, (place_ref[0:1, h:h + 1] + 1).astype(F32), listed)
    out_ref[rows:, LANES:2 * LANES] = listed.astype(BF16)


def row_experts(total, columns, piece, n_expert):
    step = iota((total, columns), 0) // piece
    return step, partner(lax.axis_index("expert"), step, n_expert).astype(F32) + 1.0


def select_kernel(n_expert, n_dp, first, slots, topk, hot, *refs):
    blocks, spread_ref, earlier_ref = refs[:n_dp], refs[n_dp], refs[n_dp + 1]
    sends = refs[n_dp + 2:n_dp + 2 + n_expert]
    pick_ref, small_ref, group_ref = refs[n_dp + 2 + n_expert:]
    per = group_ref.shape[0] // n_dp
    count = per // CHUNKS
    piece = slots * CHUNKS
    total = n_expert * piece
    columns = n_dp * per
    small = None
    for j, ref in enumerate(blocks):
        group_ref[j * per:(j + 1) * per, :] = ref[:per, :]
        part = ref[per:, :LANES].astype(F32)
        small = part if small is None else small + part
    places = blocks[0][per:, LANES:2 * LANES].astype(F32)
    _, expert = row_experts(total, LANES, piece, n_expert)
    named = jnp.zeros((total, LANES), F32)
    for k in range(topk):
        named = jnp.where(small[k:k + 1, :] == expert, 1.0, named)
    rank = dot(named, earlier_ref[...])
    spread = dot(small, spread_ref[...])
    small_ref[...] = spread
    step, expert = row_experts(total, columns, piece, n_expert)
    row, col = iota((total, columns), 0), iota((total, columns), 1)
    slot = ((row - step * piece) // CHUNKS).astype(F32)
    allowed = slot < first
    for h in range(hot):
        allowed |= expert == places[h:h + 1, :1]
    hit = None
    for k in range(topk):
        same = spread[k:k + 1, :] == expert
        hit = same if hit is None else hit | same
    chunk = row % CHUNKS == (col % per) // count
    pick = onehot(hit & allowed & chunk & (rank == slot))
    pick_ref[...] = pick
    value = mm(pick, group_ref[...]).astype(BF16)
    for j, ref in enumerate(sends):
        ref[...] = value[j * piece:(j + 1) * piece, :]


def expert_kernel(steps, *refs):
    ins, outs = refs[:steps], refs[steps + 4:2 * steps + 4]
    gate_ref, up_ref, down_ref, order_ref = refs[steps:steps + 4]
    x_ref, y_ref = refs[2 * steps + 4:]
    total, lanes = y_ref.shape
    piece = total // steps
    count = total // CHUNKS
    nt = ((1,), (1,))
    for j, ref in enumerate(ins):
        y_ref[j * piece:(j + 1) * piece, :] = ref[...]
    x = mm(order_ref[...], y_ref[...]).astype(BF16)
    for c in range(CHUNKS):
        x_ref[:, c * lanes:(c + 1) * lanes] = x[c * count:(c + 1) * count, :]
    gate = mm(gate_ref[...], x_ref[...], nt)
    up = mm(up_ref[...], x_ref[...], nt)
    hidden = (gate / (1.0 + jnp.exp(-gate)) * up).T.astype(BF16)
    for c in range(CHUNKS):
        value = mm(hidden, down_ref[:, c * lanes:(c + 1) * lanes]).astype(BF16)
        y_ref[c * count:(c + 1) * count, :] = value
    y = mm(order_ref[...], y_ref[...], ((0,), (0,))).astype(BF16)
    for j, ref in enumerate(outs):
        ref[...] = y[j * piece:(j + 1) * piece, :]


def mix_kernel(steps, *refs):
    backs, mix_ref, out_refs, rows_ref = refs[:steps], refs[steps], refs[steps + 1:-1], refs[-1]
    piece = backs[0].shape[0]
    for j, ref in enumerate(backs):
        rows_ref[j * piece:(j + 1) * piece, :] = ref[...]
    value = mm(mix_ref[...], rows_ref[...], ((0,), (0,))).astype(BF16)
    per = out_refs[0].shape[0]
    for j, ref in enumerate(out_refs):
        ref[...] = value[j * per:(j + 1) * per, :]


def finish_kernel(*refs):
    out_ref = refs[-1]
    total = refs[0][...].astype(F32)
    for ref in refs[1:-1]:
        total += ref[...].astype(F32)
    total = total.astype(BF16)
    lanes = total.shape[1]
    count = out_ref.shape[0]
    for c in range(CHUNKS):
        out_ref[:, c * lanes:(c + 1) * lanes] = total[c * count:(c + 1) * count, :]


def call(kernel, out_shape, in_specs=None, scratch=(), limit=8 << 20, **kw):
    return pl.pallas_call(
        kernel,
        out_shape=out_shape,
        scratch_shapes=scratch,
        compiler_params=pltpu.CompilerParams(vmem_limit_bytes=limit),
        **({} if in_specs is None else {"in_specs": in_specs}),
        **kw,
    )


def in_hbm(x):
    return pltpu.with_memory_space_constraint(x, pltpu.HBM)


def fetch_kernel(n_expert, topk, *refs):
    ins, pick_ref, small_ref, outs, order_ref, mix_ref, sems = (
        refs[:3], refs[3], refs[4], refs[5:8], refs[8], refs[9], refs[10]
    )
    copies = []
    for i, (a, b) in enumerate(zip(ins, outs)):
        part = a.shape[0] // PARTS
        for p in range(PARTS):
            rows = pl.ds(p * part, part)
            copies.append(pltpu.make_async_copy(a.at[rows], b.at[rows], sems.at[i * PARTS + p]))
    for copy in copies:
        copy.start()
    total, columns = pick_ref.shape
    count = total // CHUNKS
    row, col = iota((total, total), 0), iota((total, total), 1)
    order_ref[...] = onehot(col == (row % count) * CHUNKS + row // count)
    _, expert = row_experts(total, columns, total // n_expert, n_expert)
    gate = jnp.zeros((total, columns), F32)
    for k in range(topk):
        hit = small_ref[k:k + 1, :] == expert
        gate = jnp.where(hit, small_ref[topk + k:topk + k + 1, :], gate)
    mix_ref[...] = jnp.where(pick_ref[...].astype(F32) > 0.0, gate, 0.0).astype(BF16)
    for copy in copies:
        copy.wait()


def body(tokens, expert_ids, gate_weights, placement, w_gate, w_up, w_down):
    n_expert, n_dp = lax.axis_size("expert"), lax.axis_size("dp")
    count, width = tokens.shape
    topk = expert_ids.shape[1]
    group = count * n_dp
    assert group <= LANES and w_gate.shape[1] % (16 * PARTS) == 0 and n_expert < 256 and width % (CHUNKS * LANES) == 0
    assert width >= 2 * CHUNKS * LANES and placement.shape[1] <= 8
    first = max(2, group * topk // n_expert)
    slots = first + max(1, first // 2)
    lanes = width // CHUNKS
    per = count * CHUNKS
    extra = -(-2 * topk // 8) * 8
    total = n_expert * slots * CHUNKS
    shape = lambda *dims: jax.ShapeDtypeStruct(dims, BF16)
    hbm = pl.BlockSpec(memory_space=pltpu.HBM)
    big = total > 1024

    columns = n_dp * per
    table = shape(LANES, columns)
    packed, spread, earlier = call(
        pack_kernel,
        [shape(per + extra, lanes), table, table],
        [hbm] * 4,
        (
            pltpu.VMEM((count, width), BF16),
            pltpu.VMEM((topk, count), I32),
            pltpu.VMEM((topk, count), BF16),
            pltpu.VMEM(placement.shape, I32),
            pltpu.SemaphoreType.DMA((4,)),
        ),
    )(*map(in_hbm, (tokens, expert_ids.T, gate_weights.T, placement)))
    blocks = swap([packed] * n_dp, "dp")
    hot = placement.shape[1]
    *sends, pick, small = call(
        functools.partial(select_kernel, n_expert, n_dp, first, slots, topk, hot),
        [shape(slots * CHUNKS, lanes)] * n_expert
        + [shape(total, columns), jax.ShapeDtypeStruct((extra, columns), F32)],
        scratch=(pltpu.VMEM((columns, lanes), BF16),),
        limit=48 << 20 if big else 8 << 20,
    )(*blocks, spread, earlier)
    weights = [w[0] for w in (w_gate, w_up, w_down)]
    vmem = pl.BlockSpec(memory_space=pltpu.VMEM)
    *weights, order, mix = call(
        functools.partial(fetch_kernel, n_expert, topk),
        [shape(*w.shape) for w in weights] + [shape(total, total), shape(total, columns)],
        [hbm] * 3 + [vmem] * 2,
        (pltpu.SemaphoreType.DMA((3 * PARTS,)),),
        limit=48 << 20 if big else 16 << 20,
        cost_estimate=pl.CostEstimate(
            flops=0, bytes_accessed=sum(4 * w.size for w in weights), transcendentals=0
        ),
    )(*map(in_hbm, weights), pick, small)
    rows = swap(sends, "expert")
    parts = call(
        functools.partial(expert_kernel, n_expert),
        [shape(slots * CHUNKS, lanes)] * n_expert,
        scratch=(
            pltpu.VMEM((total // CHUNKS, width), BF16),
            pltpu.VMEM((total, lanes), BF16),
        ),
        limit=60 << 20 if big else 24 << 20,
    )(*rows, *weights, order)
    backs = swap(parts, "expert")
    outs = call(
        functools.partial(mix_kernel, n_expert),
        [shape(per, lanes)] * n_dp,
        scratch=(pltpu.VMEM((total, lanes), BF16),),
        limit=32 << 20 if big else 8 << 20,
    )(*backs, mix)
    pieces = swap(outs, "dp")
    return call(finish_kernel, shape(count, width))(*pieces)


def solution(mesh):
    placed = (
        P(("groups", "expert", "dp"), None),
        P(("groups", "expert", "dp"), None),
        P(("groups", "expert", "dp"), None),
        P("groups", None),
        P("expert", "dp", None),
        P("expert", "dp", None),
        P("expert", "dp", None),
    )
    return jax.shard_map(
        body,
        mesh=mesh,
        in_specs=placed,
        out_specs=P(("groups", "expert", "dp"), None),
        check_vma=False,
    )
```

```python
import functools

import jax
import jax.numpy as jnp
from jax import lax
from jax.experimental import pallas as pl
from jax.experimental.pallas import tpu as pltpu
from jax.sharding import PartitionSpec as P


BF16, F32, I32 = jnp.bfloat16, jnp.float32, jnp.int32
CHUNKS = 8
LANES = 128
PARTS = 4


def iota(shape, dim):
    return lax.broadcasted_iota(I32, shape, dim)


def onehot(cond):
    return jnp.where(cond, 1.0, 0.0).astype(BF16)


def mm(a, b, contract=((1,), (0,))):
    return lax.dot_general(a, b, (contract, ((), ())), preferred_element_type=F32)


def dot(a, b, contract=((1,), (0,))):
    return mm(a.astype(BF16), b.astype(BF16), contract)


def partner(me, step, n):
    if n & (n - 1) == 0:
        return me ^ step
    return (step + n - me) % n


def swap(xs, axis):
    n = lax.axis_size(axis)
    out = []
    for j, x in enumerate(xs):
        pairs = [(i, partner(i, j, n)) for i in range(n)]
        out.append(lax.ppermute(x, axis, pairs) if j else x)
    return out


def pack_kernel(tok_hbm, ids_hbm, gate_hbm, place_hbm, *refs):
    out_ref, spread_ref, earlier_ref, tok_ref, ids_ref, gate_ref, place_ref, sems = refs
    pairs = ((ids_hbm, ids_ref), (gate_hbm, gate_ref), (place_hbm, place_ref), (tok_hbm, tok_ref))
    copies = [pltpu.make_async_copy(a, b, sems.at[i]) for i, (a, b) in enumerate(pairs)]
    for copy in copies:
        copy.start()
    count, width = tok_ref.shape
    topk = ids_ref.shape[0]
    lanes = width // CHUNKS
    rows = count * CHUNKS
    extra = out_ref.shape[0] - rows
    me = lax.axis_index("dp")
    columns = spread_ref.shape[1]
    at = iota((LANES, columns), 1)
    token = partner(me, at // rows, columns // rows) * count + at % count
    spread_ref[...] = onehot(iota((LANES, columns), 0) == token)
    earlier_ref[...] = onehot(iota((LANES, columns), 0) < token)
    place = onehot(iota((count, LANES), 1) == iota((count, LANES), 0) + me * count)
    ids_row = onehot(iota((extra, topk), 0) == iota((extra, topk), 1))
    gate_row = onehot(iota((extra, topk), 0) == iota((extra, topk), 1) + topk)
    out_ref[rows:, 2 * LANES:] = jnp.zeros((extra, lanes - 2 * LANES), BF16)
    for copy in copies:
        copy.wait()
    for c in range(CHUNKS):
        out_ref[c * count:(c + 1) * count, :] = tok_ref[:, c * lanes:(c + 1) * lanes]
    small = dot(ids_row, (ids_ref[...] + 1).astype(F32)) + dot(gate_row, gate_ref[...])
    out_ref[rows:, :LANES] = dot(small, place).astype(BF16)
    line = iota((extra, LANES), 0)
    listed = jnp.zeros((extra, LANES), F32)
    for h in range(place_ref.shape[1]):
        listed = jnp.where(line == h, (place_ref[0:1, h:h + 1] + 1).astype(F32), listed)
    out_ref[rows:, LANES:2 * LANES] = listed.astype(BF16)


def row_experts(total, columns, piece, n_expert):
    step = iota((total, columns), 0) // piece
    return step, partner(lax.axis_index("expert"), step, n_expert).astype(F32) + 1.0


def select_kernel(n_expert, n_dp, first, slots, topk, hot, *refs):
    blocks, spread_ref, earlier_ref = refs[:n_dp], refs[n_dp], refs[n_dp + 1]
    sends = refs[n_dp + 2:n_dp + 2 + n_expert]
    pick_ref, small_ref, group_ref = refs[n_dp + 2 + n_expert:]
    per = group_ref.shape[0] // n_dp
    count = per // CHUNKS
    piece = slots * CHUNKS
    total = n_expert * piece
    columns = n_dp * per
    small = None
    for j, ref in enumerate(blocks):
        group_ref[j * per:(j + 1) * per, :] = ref[:per, :]
        part = ref[per:, :LANES].astype(F32)
        small = part if small is None else small + part
    places = blocks[0][per:, LANES:2 * LANES].astype(F32)
    _, expert = row_experts(total, LANES, piece, n_expert)
    named = jnp.zeros((total, LANES), F32)
    for k in range(topk):
        named = jnp.where(small[k:k + 1, :] == expert, 1.0, named)
    rank = dot(named, earlier_ref[...])
    spread = dot(small, spread_ref[...])
    small_ref[...] = spread
    step, expert = row_experts(total, columns, piece, n_expert)
    row, col = iota((total, columns), 0), iota((total, columns), 1)
    slot = ((row - step * piece) // CHUNKS).astype(F32)
    allowed = slot < first
    for h in range(hot):
        allowed |= expert == places[h:h + 1, :1]
    hit = None
    for k in range(topk):
        same = spread[k:k + 1, :] == expert
        hit = same if hit is None else hit | same
    chunk = row % CHUNKS == (col % per) // count
    pick = onehot(hit & allowed & chunk & (rank == slot))
    pick_ref[...] = pick
    value = mm(pick, group_ref[...]).astype(BF16)
    for j, ref in enumerate(sends):
        ref[...] = value[j * piece:(j + 1) * piece, :]


def expert_kernel(pieces, *refs):
    ins, outs = refs[:pieces], refs[pieces + 4:2 * pieces + 4]
    gate_ref, up_ref, down_ref, order_ref = refs[pieces:pieces + 4]
    x_ref, rows_ref = refs[2 * pieces + 4:]
    piece, lanes = ins[0].shape
    count = x_ref.shape[0]
    for j, ref in enumerate(ins):
        rows_ref[j * piece:(j + 1) * piece, :] = ref[...]
    x = mm(order_ref[...], rows_ref[...]).astype(BF16)
    for c in range(CHUNKS):
        x_ref[:, c * lanes:(c + 1) * lanes] = x[c * count:(c + 1) * count, :]
    gate = mm(x_ref[...], gate_ref[...])
    up = mm(x_ref[...], up_ref[...])
    hidden = (gate / (1.0 + jnp.exp(-gate)) * up).astype(BF16)
    for c in range(CHUNKS):
        value = mm(hidden, down_ref[:, c * lanes:(c + 1) * lanes]).astype(BF16)
        rows_ref[c * count:(c + 1) * count, :] = value
    y = mm(order_ref[...], rows_ref[...], ((0,), (0,))).astype(BF16)
    for j, ref in enumerate(outs):
        ref[...] = y[j * piece:(j + 1) * piece, :]


def mix_kernel(steps, *refs):
    backs, mix_ref, out_refs, rows_ref = refs[:steps], refs[steps], refs[steps + 1:-1], refs[-1]
    piece = backs[0].shape[0]
    for j, ref in enumerate(backs):
        rows_ref[j * piece:(j + 1) * piece, :] = ref[...]
    value = mm(mix_ref[...], rows_ref[...], ((0,), (0,))).astype(BF16)
    per = out_refs[0].shape[0]
    for j, ref in enumerate(out_refs):
        ref[...] = value[j * per:(j + 1) * per, :]


def finish_kernel(*refs):
    out_ref = refs[-1]
    total = refs[0][...].astype(F32)
    for ref in refs[1:-1]:
        total += ref[...].astype(F32)
    total = total.astype(BF16)
    lanes = total.shape[1]
    count = out_ref.shape[0]
    for c in range(CHUNKS):
        out_ref[:, c * lanes:(c + 1) * lanes] = total[c * count:(c + 1) * count, :]


def call(kernel, out_shape, in_specs=None, scratch=(), limit=8 << 20, **kw):
    return pl.pallas_call(
        kernel,
        out_shape=out_shape,
        scratch_shapes=scratch,
        compiler_params=pltpu.CompilerParams(vmem_limit_bytes=limit),
        **({} if in_specs is None else {"in_specs": in_specs}),
        **kw,
    )


def in_hbm(x):
    return pltpu.with_memory_space_constraint(x, pltpu.HBM)


def copies_of(source, target, sems, at):
    part = source.shape[0] // PARTS
    rows = [pl.ds(p * part, part) for p in range(PARTS)]
    return [
        pltpu.make_async_copy(source.at[r], target.at[r], sems.at[at + p]) for p, r in enumerate(rows)
    ]


def turn(source, target):
    width = source.shape[1] // CHUNKS
    for c in range(CHUNKS):
        target[c * width:(c + 1) * width, :] = source[:, c * width:(c + 1) * width].T


def fetch_kernel(gate_hbm, up_hbm, gate_ref, up_ref, order_ref, held, sems):
    first = copies_of(gate_hbm, held, sems, 0)
    second = copies_of(up_hbm, up_ref, sems, PARTS)
    for copy in first + second:
        copy.start()
    total = order_ref.shape[0]
    count = total // CHUNKS
    row, col = iota((total, total), 0), iota((total, total), 1)
    order_ref[...] = onehot(col == (row % count) * CHUNKS + row // count)
    for copy in first:
        copy.wait()
    turn(held, gate_ref)
    for copy in second:
        copy.wait()


def prepare_kernel(n_expert, topk, up_ref, down_hbm, pick_ref, small_ref, *refs):
    turned_ref, down_ref, mix_ref, sems = refs
    copies = copies_of(down_hbm, down_ref, sems, 0)
    for copy in copies:
        copy.start()
    turn(up_ref, turned_ref)
    total, columns = pick_ref.shape
    _, expert = row_experts(total, columns, total // n_expert, n_expert)
    gate = jnp.zeros((total, columns), F32)
    for k in range(topk):
        hit = small_ref[k:k + 1, :] == expert
        gate = jnp.where(hit, small_ref[topk + k:topk + k + 1, :], gate)
    mix_ref[...] = jnp.where(pick_ref[...].astype(F32) > 0.0, gate, 0.0).astype(BF16)
    for copy in copies:
        copy.wait()


def body(tokens, expert_ids, gate_weights, placement, w_gate, w_up, w_down):
    n_expert, n_dp = lax.axis_size("expert"), lax.axis_size("dp")
    count, width = tokens.shape
    topk = expert_ids.shape[1]
    group = count * n_dp
    assert group <= LANES and w_gate.shape[1] % (16 * PARTS) == 0 and n_expert < 256 and width % (CHUNKS * LANES) == 0
    assert width >= 2 * CHUNKS * LANES and placement.shape[1] <= 8
    first = max(2, group * topk // n_expert)
    slots = first + max(1, first // 2)
    lanes = width // CHUNKS
    per = count * CHUNKS
    extra = -(-2 * topk // 8) * 8
    total = n_expert * slots * CHUNKS
    shape = lambda *dims: jax.ShapeDtypeStruct(dims, BF16)
    hbm = pl.BlockSpec(memory_space=pltpu.HBM)
    big = total > 1024

    columns = n_dp * per
    table = shape(LANES, columns)
    packed, spread, earlier = call(
        pack_kernel,
        [shape(per + extra, lanes), table, table],
        [hbm] * 4,
        (
            pltpu.VMEM((count, width), BF16),
            pltpu.VMEM((topk, count), I32),
            pltpu.VMEM((topk, count), BF16),
            pltpu.VMEM(placement.shape, I32),
            pltpu.SemaphoreType.DMA((4,)),
        ),
    )(*map(in_hbm, (tokens, expert_ids.T, gate_weights.T, placement)))
    blocks = swap([packed] * n_dp, "dp")
    hot = placement.shape[1]
    *sends, pick, small = call(
        functools.partial(select_kernel, n_expert, n_dp, first, slots, topk, hot),
        [shape(slots * CHUNKS, lanes)] * n_expert
        + [shape(total, columns), jax.ShapeDtypeStruct((extra, columns), F32)],
        scratch=(pltpu.VMEM((columns, lanes), BF16),),
        limit=48 << 20 if big else 8 << 20,
    )(*blocks, spread, earlier)
    vmem = pl.BlockSpec(memory_space=pltpu.VMEM)
    piece = slots * CHUNKS
    block = w_gate.shape[1:]
    turned = shape(*block[::-1])
    gate, up, order = call(
        fetch_kernel,
        [turned, shape(*block), shape(total, total)],
        [hbm] * 2,
        (pltpu.VMEM(block, BF16), pltpu.SemaphoreType.DMA((2 * PARTS,))),
        limit=48 << 20 if big else 16 << 20,
    )(in_hbm(w_gate[0]), in_hbm(w_up[0]))
    up, down, mix = call(
        functools.partial(prepare_kernel, n_expert, topk),
        [turned, shape(*block), shape(total, columns)],
        [vmem, hbm, vmem, vmem],
        (pltpu.SemaphoreType.DMA((PARTS,)),),
        limit=48 << 20 if big else 16 << 20,
    )(up, in_hbm(w_down[0]), pick, small)
    rows = swap(sends, "expert")
    parts = call(
        functools.partial(expert_kernel, n_expert),
        [shape(piece, lanes)] * n_expert,
        scratch=(
            pltpu.VMEM((total // CHUNKS, width), BF16),
            pltpu.VMEM((total, lanes), BF16),
        ),
        limit=60 << 20 if big else 24 << 20,
    )(*rows, gate, up, down, order)
    backs = swap(parts, "expert")
    outs = call(
        functools.partial(mix_kernel, n_expert),
        [shape(per, lanes)] * n_dp,
        scratch=(pltpu.VMEM((total, lanes), BF16),),
        limit=32 << 20 if big else 8 << 20,
    )(*backs, mix)
    pieces = swap(outs, "dp")
    return call(finish_kernel, shape(count, width))(*pieces)


def solution(mesh):
    placed = (
        P(("groups", "expert", "dp"), None),
        P(("groups", "expert", "dp"), None),
        P(("groups", "expert", "dp"), None),
        P("groups", None),
        P("expert", "dp", None),
        P("expert", "dp", None),
        P("expert", "dp", None),
    )
    return jax.shard_map(
        body,
        mesh=mesh,
        in_specs=placed,
        out_specs=P(("groups", "expert", "dp"), None),
        check_vma=False,
    )
```
